512 devices in a mesh: line: 64 (over z, x, core), span: 8 (over y).
Axes of the slice: x: 4, y: 8, z: 8, core: 2. Of those that a mesh axis runs over, the one named last changes fastest.
Arguments:
- jacobian: bfloat16 [5, 5, 8, 4096, 128], P(None, None, 'span', 'line'), may hold values from -1 to 1
- state: float32 [5, 8, 4096, 128], P(None, 'span', 'line'), may hold values from -6 to 6
- metric: float32 [8, 4096, 128], P('span', 'line'), may hold values from 0.5 to 1.5
- dissipation: float32 [8, 4096, 128], P('span', 'line'), may hold values from 2 to 10
- time_term: float32 [8, 4096, 128], P('span', 'line'), may hold values from 0.0001 to 0.0005
Outputs:
- update: float32 [5, 8, 4096, 128], P(None, 'span', 'line')
The draws below stay inside these ranges and needn't reach their ends.
All inputs are finite; a program needn't handle non-finite values.
Results may differ from the reference program's by a relative error of at most 0.0003.
Values sent between devices are 32-bit elements; how exact they have to be, the bound alone decides.
A program may use at most 64 MiB of HBM per device.

```python
import math
import jax
import jax.numpy as jnp
from jax import lax

NVAR = 5
LINES = 128
NX = 4096
NS = 8


def draw_jacobian(key, part):
    base_key = jax.random.fold_in(key, 11)
    sign_key = jax.random.fold_in(key, 12)
    mag_key = jax.random.fold_in(key, 13)
    noise_key = jax.random.fold_in(key, 14)
    off_part = jnp.clip(0.07 * jax.random.normal(base_key, (NVAR, NVAR), jnp.float32), -0.15, 0.15)
    signs = jnp.where(jax.random.bernoulli(sign_key, 0.5, (NVAR,)), 1.0, -1.0).astype(jnp.float32)
    magnitudes = jax.random.uniform(mag_key, (NVAR,), jnp.float32, 0.4, 0.8)
    unit_matrix = jnp.eye(NVAR, dtype=jnp.float32)
    base = off_part * (1.0 - unit_matrix) + unit_matrix * (signs * magnitudes)[:, None]
    shape = (NVAR, NVAR, NS, NX, LINES)
    noise = jnp.clip(0.1 * jax.random.normal(noise_key, shape, jnp.float32), -0.2, 0.2)
    return (base[:, :, None, None, None] + noise).astype(jnp.bfloat16)


def shard_levels(rng, shape, cuts, smallest, largest):
    def one(axis_at, blocks):
        draws = jax.random.uniform(jax.random.fold_in(jax.random.fold_in(rng, 6), axis_at), (blocks,), jnp.float32, smallest / len(cuts), largest / len(cuts))
        return jnp.repeat(jnp.exp(draws), shape[axis_at] // blocks).reshape((-1,) + (1,) * (len(shape) - axis_at - 1))

    level = one(*cuts[0])
    for cut in cuts[1:]:
        level = level * one(*cut)
    return level


def bell_draw(stream_key, dims, width, most, shards=(), kind=jnp.bfloat16):
    drawn = width * jax.random.normal(stream_key, dims, jnp.float32)
    if shards:
        drawn = drawn * shard_levels(stream_key, dims, shards, -0.22, 0.18)
    return jnp.clip(drawn, -most, most).astype(kind)


def setup_inputs(seed: int = 0) -> dict:
    seeds = jax.random.split(jax.random.key(seed), 6)
    return {
        "jacobian": draw_jacobian(jax.random.fold_in(seeds[5], 71), 0),
        "state": bell_draw(seeds[1], (NVAR, NS, NX, LINES), 1.0, 6.0, ((1, 8), (2, 64)), jnp.float32),
        "metric": jnp.clip(jnp.exp(math.log(1.5) - 1.0986123 * jax.random.uniform(seeds[2], (NS, NX, LINES), jnp.float32) ** shard_levels(seeds[2], (NS, NX, LINES), ((0, 8), (1, 64)), -0.2, 0.2)), 0.5, 1.5),
        "dissipation": jnp.clip(jnp.exp(math.log(10.0) - 1.609438 * jax.random.uniform(seeds[3], (NS, NX, LINES), jnp.float32) ** shard_levels(seeds[3], (NS, NX, LINES), ((0, 8), (1, 64)), -0.2, 0.2)), 2.0, 10.0),
        "time_term": jnp.clip(jnp.exp(math.log(0.0005) - 1.609438 * jax.random.uniform(seeds[4], (NS, NX, LINES), jnp.float32) ** shard_levels(seeds[4], (NS, NX, LINES), ((0, 8), (1, 64)), -0.2, 0.2)), 0.0001, 0.0005),
    }


span_weight = 0.25
highest = lax.Precision.HIGHEST

def build_system(jacobian, state, metric, dissipation, time_term):
    jac_float = jacobian.astype(jnp.float32)
    symmetric = 0.5 * (jac_float + jnp.swapaxes(jac_float, 0, 1))
    flux_matrix = metric[None, None] * symmetric
    flux_term = jnp.einsum('ijsxn,jsxn->isxn', flux_matrix, state, precision=highest)
    padded_flux = jnp.pad(flux_term, ((0, 0), (0, 0), (1, 1), (0, 0)))
    padded_planes = jnp.pad(state, ((0, 0), (1, 1), (0, 0), (0, 0)))
    residual = -0.5 * (padded_flux[:, :, 2:] - padded_flux[:, :, :-2])
    residual = residual + span_weight * (padded_planes[:, 2:] - 2.0 * state + padded_planes[:, :-2])
    padded_diss = jnp.pad(dissipation, ((0, 0), (1, 1), (0, 0)))
    face_lo = 0.5 * (padded_diss[:, :-2] + dissipation)
    face_hi = 0.5 * (dissipation + padded_diss[:, 2:])
    padded_matrix = jnp.pad(flux_matrix, ((0, 0), (0, 0), (0, 0), (1, 1), (0, 0)))
    jac_lo = 0.5 * (padded_matrix[:, :, :, :-2] + flux_matrix)
    jac_hi = 0.5 * (flux_matrix + padded_matrix[:, :, :, 2:])
    unit_five = jnp.eye(5, dtype=jnp.float32)[:, :, None, None, None]
    lower_blocks = -0.5 * jac_lo - face_lo[None, None] * unit_five
    upper_blocks = 0.5 * jac_hi - face_hi[None, None] * unit_five
    diag_scalar = time_term + face_lo + face_hi
    return (lower_blocks, diag_scalar, upper_blocks, residual)

def reference(jacobian, state, metric, dissipation, time_term):
    lower_blocks, diag_scalar, upper_blocks, residual = build_system(jacobian, state, metric, dissipation, time_term)
    nvar, planes_all, points, lines_all = residual.shape
    batch = planes_all * lines_all
    lower_t = jnp.transpose(lower_blocks, (3, 2, 4, 0, 1)).reshape(points, batch, nvar, nvar)
    upper_t = jnp.transpose(upper_blocks, (3, 2, 4, 0, 1)).reshape(points, batch, nvar, nvar)
    diag_t = jnp.transpose(diag_scalar, (1, 0, 2)).reshape(points, batch)
    rhs_t = jnp.transpose(residual, (2, 1, 3, 0)).reshape(points, batch, nvar)
    unit_matrix = jnp.eye(nvar, dtype=jnp.float32)

    def forward(carried, inputs):
        prev_c, prev_d = carried
        low_block, diag_now, up_block, rhs_now = inputs
        pivot_matrix = diag_now[:, None, None] * unit_matrix - jnp.matmul(low_block, prev_c, precision=highest)
        reduced_rhs = rhs_now - jnp.matmul(low_block, prev_d[..., None], precision=highest)[..., 0]
        combined = jnp.concatenate([up_block, reduced_rhs[..., None]], axis=-1)
        solved = jnp.linalg.solve(pivot_matrix, combined)
        result_pair = (solved[..., :nvar], solved[..., nvar])
        return (result_pair, result_pair)
    start_pair = (jnp.zeros((batch, nvar, nvar), jnp.float32), jnp.zeros((batch, nvar), jnp.float32))
    final_pair, stored = lax.scan(forward, start_pair, (lower_t, diag_t, upper_t, rhs_t))

    def backward(next_value, inputs):
        c_now, d_now = inputs
        value_now = d_now - jnp.matmul(c_now, next_value[..., None], precision=highest)[..., 0]
        return (value_now, value_now)
    final_value, solution = lax.scan(backward, jnp.zeros((batch, nvar), jnp.float32), stored, reverse=True)
    solution = solution.reshape(points, planes_all, lines_all, nvar)
    return jnp.transpose(solution, (3, 1, 0, 2))
```

```python
import jax
import jax.numpy as jnp
from jax import lax
from jax.experimental import pallas as pl
from jax.experimental.pallas import tpu as pltpu
from jax.sharding import PartitionSpec as P

MESH = pl.DeviceIdType.MESH
f32 = jnp.float32
span_weight = 0.25
NV = 5
GROUP = 8
WIDE = 16
PACKS = 14
PAIRS = [(i, j) for i in range(NV) for j in range(i, NV)]
SYM = [[PAIRS.index((min(i, j), max(i, j))) for j in range(NV)] for i in range(NV)]
NSYM = len(PAIRS)


def roll(x, shift, axis):
    return pltpu.roll(x, shift, axis)


def mm(left, right):
    out = []
    for i in range(NV):
        acc = left[i][0][None] * right[0]
        for k in range(1, NV):
            acc = acc + left[i][k][None] * right[k]
        out.append(acc)
    return out


def inverse(m):
    m = [list(row) for row in m]
    for p in range(NV):
        r = 1.0 / m[p][p]
        for j in range(NV):
            if j != p:
                m[p][j] = m[p][j] * r
        for i in range(NV):
            if i != p:
                f = m[i][p]
                for j in range(NV):
                    if j != p:
                        m[i][j] = m[i][j] - f * m[p][j]
                m[i][p] = -(f * r)
        m[p][p] = r
    return m


def tree_up(seg, la_ref, fb_ref, axis, size, base):
    def body(level, carry):
        back = size - lax.shift_left(jnp.int32(base), level)
        fa = [seg[0, i] for i in range(NV)]
        la = [seg[1, i] for i in range(NV)]
        fb = [roll(x, back, axis) for x in fa]
        lb = [roll(x, back, axis) for x in la]
        t = mm([[la[i][NV + k] for k in range(NV)] for i in range(NV)], fb)
        eye = [[(1.0 if i == k else 0.0) - t[i][k] for k in range(NV)] for i in range(NV)]
        x = inverse(eye)
        q = [
            jnp.concatenate(
                [la[i][0:NV], -t[i][NV : 2 * NV], la[i][2 * NV :] - t[i][2 * NV :]], axis=0
            )
            for i in range(NV)
        ]
        ela = mm(x, q)
        r = mm([[fb[i][k] for k in range(NV)] for i in range(NV)], ela)
        efb = [
            jnp.concatenate([-r[i][0:NV], fb[i][NV:] - r[i][NV:]], axis=0) for i in range(NV)
        ]
        s = mm([[fa[i][NV + k] for k in range(NV)] for i in range(NV)], efb)
        y = mm([[lb[i][k] for k in range(NV)] for i in range(NV)], ela)
        for i in range(NV):
            la_ref[level, i] = ela[i]
            fb_ref[level, i] = efb[i]
            seg[0, i, 0:NV] = fa[i][0:NV] - s[i][0:NV]
            seg[0, i, NV : 2 * NV] = -s[i][NV : 2 * NV]
            seg[0, i, 2 * NV :] = fa[i][2 * NV :] - s[i][2 * NV :]
            seg[1, i, 0:NV] = -y[i][0:NV]
            seg[1, i, NV:] = lb[i][NV:] - y[i][NV:]
        return carry

    lax.fori_loop(0, 3, body, 0)


def tree_down(p, n, la_ref, fb_ref, axis, base, pos):
    for level in (2, 1, 0):
        shift = base << level
        pn = jnp.concatenate([p, n], axis=0)
        la = []
        fb = []
        for i in range(NV):
            la.append(
                la_ref[level, i, 2 * NV :]
                - jnp.sum(la_ref[level, i, 0 : 2 * NV] * pn, axis=0, keepdims=True)
            )
            fb.append(
                fb_ref[level, i, 2 * NV :]
                - jnp.sum(fb_ref[level, i, 0 : 2 * NV] * pn, axis=0, keepdims=True)
            )
        la = jnp.concatenate(la, axis=0)
        fb = jnp.concatenate(fb, axis=0)
        second = (pos & shift) != 0
        p, n = (
            jnp.where(second, roll(la, shift, axis), p),
            jnp.where(second, roll(n, shift, axis), fb),
        )
    return p, n


def swap_blocks(x):
    sub = lax.broadcasted_iota(jnp.int32, x.shape, 1)
    lane = lax.broadcasted_iota(jnp.int32, x.shape, 2)
    for bit in range(3):
        j = lax.shift_right_logical(sub, bit) & 1
        k = lax.shift_right_logical(lane, 4 + bit) & 1
        s = 1 << bit
        w = WIDE << bit
        up = roll(roll(x, GROUP - s, 1), w, 2)
        down = roll(roll(x, s, 1), 128 - w, 2)
        x = jnp.where(j == k, x, jnp.where(j == 0, up, down))
    return x


def kernel(
    jac_ref, state_ref, metric_ref, diss_ref, time_ref, out_ref,
    sym_ref, flux_ref, fst, dst, xst, ls, us, fs,
    rim_out, rim_in, span_in,
    wc, pinv, hg, es,
    seg1, la1, fb1, seg2, la2, fb2, seg3, la3, fb3,
    tmp, a_out, a_in, b_out, b_in, c_out, c_in,
    span_sem, rim_sem, a_sem, b_sem, c_sem,
):
    line = lax.axis_index("line")
    span = lax.axis_index("span")
    n_line = lax.axis_size("line")
    n_span = lax.axis_size("span")
    plane = line // GROUP
    member = line % GROUP
    line_next = lax.rem(line + 1, n_line)
    line_prev = lax.rem(line + n_line - 1, n_line)
    span_next = lax.rem(span + 1, n_span)
    span_prev = lax.rem(span + n_span - 1, n_span)
    members = [plane * GROUP + lax.rem(member + o, GROUP) for o in range(1, GROUP)]
    planes = [lax.rem(plane + o, GROUP) * GROUP + member for o in range(1, GROUP)]

    peers = [(line, span_next), (line, span_prev), (line_next, span), (line_prev, span)]
    peers += [(x, span) for x in members] + [(x, span) for x in planes]
    barrier = pltpu.get_barrier_semaphore()
    for peer in peers:
        pl.semaphore_signal(barrier, inc=1, device_id=peer, device_id_type=MESH)

    metric = metric_ref[...]
    for q, (i, j) in enumerate(PAIRS):
        if i == j:
            value = jac_ref[i, i].astype(f32)
        else:
            value = 0.5 * (jac_ref[i, j].astype(f32) + jac_ref[j, i].astype(f32))
        sym_ref[q] = metric * value
    for i in range(NV):
        acc = sym_ref[SYM[i][0]] * state_ref[0]
        for k in range(1, NV):
            acc = acc + sym_ref[SYM[i][k]] * state_ref[k]
        flux_ref[i] = acc
    points = metric.shape[0]
    for side, row in ((0, points - 1), (1, 0)):
        for q in range(NSYM):
            rim_out[side, q : q + 1, :] = sym_ref[q, row : row + 1, :]
        for i in range(NV):
            rim_out[side, NSYM + i : NSYM + i + 1, :] = flux_ref[i, row : row + 1, :]
        rim_out[side, NSYM + NV : NSYM + NV + 1, :] = diss_ref[row : row + 1, :]
        rim_out[side, NSYM + NV + 1 :, :] = jnp.zeros((24 - NSYM - NV - 1, 128), f32)

    pl.semaphore_wait(barrier, len(peers))

    copies_rim = []
    for side, target in ((0, line_next), (1, line_prev)):
        copies_rim.append(
            pltpu.make_async_remote_copy(
                src_ref=rim_out.at[side], dst_ref=rim_in.at[side],
                send_sem=rim_sem.at[0, side], recv_sem=rim_sem.at[1, side],
                device_id=(target, span), device_id_type=MESH,
            )
        )
        copies_rim[-1].start()
    copies_span = []
    for side, target in ((0, span_next), (1, span_prev)):
        copies_span.append(
            pltpu.make_async_remote_copy(
                src_ref=state_ref, dst_ref=span_in.at[side],
                send_sem=span_sem.at[0, side], recv_sem=span_sem.at[1, side],
                device_id=(line, target), device_id_type=MESH,
            )
        )
        copies_span[-1].start()

    for t in range(GROUP):
        fst[t + 1] = sym_ref[:, pl.ds(t, GROUP, stride=GROUP), :]
        xst[t + 1] = flux_ref[:, pl.ds(t, GROUP, stride=GROUP), :]
        dst[t + 1] = diss_ref[pl.ds(t, GROUP, stride=GROUP), :]
    sub3 = lax.broadcasted_iota(jnp.int32, (1, GROUP, 128), 1)
    sub2 = lax.broadcasted_iota(jnp.int32, (GROUP, 128), 0)
    for c in copies_rim:
        c.wait()
    first_device = line == 0
    last_device = line == n_line - 1
    for side, at, source, turn, edge, outside in (
        (0, 0, GROUP, 1, 0, first_device),
        (1, GROUP + 1, 1, GROUP - 1, GROUP - 1, last_device),
    ):
        rim = jnp.where(outside, 0.0, rim_in[side])
        for q in range(NSYM):
            fst[at, q] = jnp.where(sub2 == edge, rim[q : q + 1, :], roll(fst[source, q], turn, 0))
        for i in range(NV):
            xst[at, i] = jnp.where(
                sub2 == edge, rim[NSYM + i : NSYM + i + 1, :], roll(xst[source, i], turn, 0)
            )
        dst[at] = jnp.where(
            sub2 == edge, rim[NSYM + NV : NSYM + NV + 1, :], roll(dst[source], turn, 0)
        )

    def faces(t, carry):
        g = 0.25 * (fst[t] + fst[t + 1])
        f = 0.5 * (dst[t] + dst[t + 1])
        fs[t] = f
        for i in range(NV):
            for k in range(NV):
                e = g[SYM[i][k]]
                us[t, i, k] = e - f if i == k else e
                ls[t, i, k] = -e - f if i == k else -e
        return carry

    lax.fori_loop(0, GROUP + 1, faces, 0)

    zero = jnp.zeros((GROUP, 128), f32)
    for i in range(NV):
        for k in range(2 * NV):
            wc[0, i, k] = zero - 1.0 if i == k else zero
    for t in range(GROUP):
        dst[t] = fs[t] + time_ref[pl.ds(t, GROUP, stride=GROUP), :] + fs[t + 1]

    def forward(t, carry):
        diag = dst[t]
        low = [[ls[t, i, k] for k in range(NV)] for i in range(NV)]
        prod = mm(low, [wc[t, i] for i in range(NV)])
        m = [
            [(diag - prod[i][NV + k]) if i == k else -prod[i][NV + k] for k in range(NV)]
            for i in range(NV)
        ]
        inv = inverse(m)
        for i in range(NV):
            for k in range(NV):
                pinv[t, k, i] = inv[i][k]
        w = mm(inv, [-prod[i][0:NV] for i in range(NV)])
        c = mm(inv, [us[t + 1, i] for i in range(NV)])
        for i in range(NV):
            wc[t + 1, i, 0:NV] = w[i]
            wc[t + 1, i, NV:] = c[i]
        return carry

    lax.fori_loop(0, GROUP, forward, 0)

    for i in range(NV):
        hg[GROUP - 1, i] = wc[GROUP, i]

    def spikes(step, carry):
        t = GROUP - 2 - step
        c = [[wc[t + 1, i, NV + k] for k in range(NV)] for i in range(NV)]
        prod = mm(c, [hg[t + 1, i] for i in range(NV)])
        for i in range(NV):
            hg[t, i, 0:NV] = wc[t + 1, i, 0:NV] - prod[i][0:NV]
            hg[t, i, NV:] = -prod[i][NV:]
        return carry

    lax.fori_loop(0, GROUP - 1, spikes, 0)

    for c in copies_span:
        c.wait()
    no_prev = span == 0
    no_next = span == n_span - 1
    d = jnp.zeros((NV, GROUP, 128), f32)
    for t in range(GROUP):
        rows = pl.ds(t, GROUP, stride=GROUP)
        before = jnp.where(no_prev, 0.0, span_in[0, :, rows, :])
        after = jnp.where(no_next, 0.0, span_in[1, :, rows, :])
        rhs = -0.5 * (xst[t + 2] - xst[t])
        rhs = rhs + span_weight * (after - 2.0 * state_ref[:, rows, :] + before)
        for k in range(NV):
            rhs = rhs - ls[t, k] * d[k][None]
        d = pinv[t, 0] * rhs[0][None]
        for k in range(1, NV):
            d = d + pinv[t, k] * rhs[k][None]
        es[t] = d
    e = d
    for t in range(GROUP - 2, -1, -1):
        rows = [
            es[t, i] - jnp.sum(wc[t + 1, i, NV:] * e, axis=0) for i in range(NV)
        ]
        for i in range(NV):
            es[t, i] = rows[i]
        e = es[t]

    for which, t in ((0, 0), (1, GROUP - 1)):
        for i in range(NV):
            seg1[which, i, 0 : 2 * NV] = hg[t, i]
            seg1[which, i, 2 * NV] = es[t, i]
    tree_up(seg1, la1, fb1, 1, GROUP, 1)

    def two_port_rows(seg):
        for which in range(2):
            for i in range(NV):
                for c in range(2 * NV + 1):
                    r = (which * NV + i) * (2 * NV + 1) + c
                    tmp[r // 8, r % 8 : r % 8 + 1, :] = seg[which, i, c, 0:1, :]

    def two_port_load(seg, landed):
        for s in range(GROUP):
            for r in range(PACKS):
                tmp[r, s : s + 1, :] = landed[s, r]
        packed = swap_blocks(tmp[...])
        for which in range(2):
            for i in range(NV):
                for c in range(2 * NV + 1):
                    r = (which * NV + i) * (2 * NV + 1) + c
                    seg[which, i, c] = packed[r // 8, r % 8 : r % 8 + 1, :]

    for r in (110, 111):
        tmp[r // 8, r % 8 : r % 8 + 1, :] = jnp.zeros((1, 128), f32)
    two_port_rows(seg1)
    packed = swap_blocks(tmp[...])
    for s in range(GROUP):
        for r in range(PACKS):
            a_out[s, r] = packed[r, s : s + 1, :]
    copies = []
    for o in range(1, GROUP):
        copies.append(
            pltpu.make_async_remote_copy(
                src_ref=a_out.at[lax.rem(member + o, GROUP)], dst_ref=a_in.at[member],
                send_sem=a_sem.at[0, o], recv_sem=a_sem.at[1, o],
                device_id=(members[o - 1], span), device_id_type=MESH,
            )
        )
        copies[-1].start()
    a_in[member] = a_out[member]
    for c in copies:
        c.wait()
    two_port_load(seg2, a_in)
    tree_up(seg2, la2, fb2, 2, 128, WIDE)

    two_port_rows(seg2)
    packed = swap_blocks(tmp[...])
    for r in range(PACKS):
        b_out[r] = packed[r, 0:1, :]
    copies = []
    for o in range(1, GROUP):
        copies.append(
            pltpu.make_async_remote_copy(
                src_ref=b_out, dst_ref=b_in.at[plane],
                send_sem=b_sem.at[0, o], recv_sem=b_sem.at[1, o],
                device_id=(planes[o - 1], span), device_id_type=MESH,
            )
        )
        copies[-1].start()
    b_in[plane] = b_out[...]
    for c in copies:
        c.wait()
    two_port_load(seg3, b_in)
    tree_up(seg3, la3, fb3, 2, 128, WIDE)

    lane = lax.broadcasted_iota(jnp.int32, (NV, 1, 128), 2)
    nothing = jnp.zeros((NV, 1, 128), f32)
    p, n = tree_down(nothing, nothing, la3, fb3, 2, WIDE, lane)
    own = lax.rem(128 - plane * WIDE, 128)
    p = roll(p, own, 2)
    n = roll(n, own, 2)
    p, n = tree_down(p, n, la2, fb2, 2, WIDE, lane)

    for i in range(NV):
        tmp[0, i : i + 1, :] = p[i]
        tmp[1, i : i + 1, :] = n[i]
    packed = swap_blocks(tmp[0:2])
    for s in range(GROUP):
        for r in range(2):
            c_out[s, r] = packed[r, s : s + 1, :]
    copies = []
    for o in range(1, GROUP):
        copies.append(
            pltpu.make_async_remote_copy(
                src_ref=c_out.at[lax.rem(member + o, GROUP)], dst_ref=c_in.at[member],
                send_sem=c_sem.at[0, o], recv_sem=c_sem.at[1, o],
                device_id=(members[o - 1], span), device_id_type=MESH,
            )
        )
        copies[-1].start()
    c_in[member] = c_out[member]
    for c in copies:
        c.wait()
    for s in range(GROUP):
        for r in range(2):
            tmp[r, s : s + 1, :] = c_in[s, r]
    packed = swap_blocks(tmp[0:2])
    p = jnp.concatenate(
        [jnp.broadcast_to(packed[0, i : i + 1, :], (GROUP, 128))[None] for i in range(NV)], axis=0
    )
    n = jnp.concatenate(
        [jnp.broadcast_to(packed[1, i : i + 1, :], (GROUP, 128))[None] for i in range(NV)], axis=0
    )
    pos = lax.broadcasted_iota(jnp.int32, (NV, GROUP, 128), 1)
    p, n = tree_down(p, n, la1, fb1, 1, 1, pos)
    pn = jnp.concatenate([p, n], axis=0)
    for t in range(GROUP):
        for i in range(NV):
            out_ref[i, pl.ds(t, GROUP, stride=GROUP), :] = es[t, i] - jnp.sum(
                hg[t, i] * pn, axis=0
            )


def per_device(jacobian, state, metric, dissipation, time_term):
    nv = state.shape[0]
    points, lines = metric.shape[1:]
    vmem = pl.BlockSpec(memory_space=pltpu.VMEM)
    tile = (GROUP, lines)

    def two_port(tile):
        return [
            pltpu.VMEM((2, nv, 2 * nv + 1) + tile, f32),
            pltpu.VMEM((3, nv, 2 * nv + 1) + tile, f32),
            pltpu.VMEM((3, nv, 2 * nv + 1) + tile, f32),
        ]

    update = pl.pallas_call(
        kernel,
        out_shape=jax.ShapeDtypeStruct((nv, points, lines), f32),
        in_specs=[vmem] * 5,
        out_specs=vmem,
        scratch_shapes=[
            pltpu.VMEM((NSYM, points, lines), f32),
            pltpu.VMEM((nv, points, lines), f32),
            pltpu.VMEM((GROUP + 2, NSYM) + tile, f32),
            pltpu.VMEM((GROUP + 2,) + tile, f32),
            pltpu.VMEM((GROUP + 2, nv) + tile, f32),
            pltpu.VMEM((GROUP + 1, nv, nv) + tile, f32),
            pltpu.VMEM((GROUP + 1, nv, nv) + tile, f32),
            pltpu.VMEM((GROUP + 1,) + tile, f32),
            pltpu.VMEM((2, 24, lines), f32),
            pltpu.VMEM((2, 24, lines), f32),
            pltpu.VMEM((2, nv, points, lines), f32),
            pltpu.VMEM((GROUP + 1, nv, 2 * nv) + tile, f32),
            pltpu.VMEM((GROUP, nv, nv) + tile, f32),
            pltpu.VMEM((GROUP, nv, 2 * nv) + tile, f32),
            pltpu.VMEM((GROUP, nv) + tile, f32),
            *two_port(tile),
            *two_port((1, lines)),
            *two_port((1, lines)),
            pltpu.VMEM((PACKS,) + tile, f32),
            pltpu.VMEM((GROUP, PACKS, 1, lines), f32),
            pltpu.VMEM((GROUP, PACKS, 1, lines), f32),
            pltpu.VMEM((PACKS, 1, lines), f32),
            pltpu.VMEM((GROUP, PACKS, 1, lines), f32),
            pltpu.VMEM((GROUP, 2, 1, lines), f32),
            pltpu.VMEM((GROUP, 2, 1, lines), f32),
            pltpu.SemaphoreType.DMA((2, 2)),
            pltpu.SemaphoreType.DMA((2, 2)),
            pltpu.SemaphoreType.DMA((2, GROUP)),
            pltpu.SemaphoreType.DMA((2, GROUP)),
            pltpu.SemaphoreType.DMA((2, GROUP)),
        ],
        compiler_params=pltpu.CompilerParams(collective_id=0, has_side_effects=True),
        name="sweep",
    )(
        jacobian.reshape((nv, nv, points, lines)),
        state.reshape((nv, points, lines)),
        metric.reshape((points, lines)),
        dissipation.reshape((points, lines)),
        time_term.reshape((points, lines)),
    )
    return update.reshape(state.shape)


def solution(mesh):
    return jax.shard_map(
        per_device,
        mesh=mesh,
        in_specs=(
            P(None, None, "span", "line", None),
            P(None, "span", "line", None),
            P("span", "line", None),
            P("span", "line", None),
            P("span", "line", None),
        ),
        out_specs=P(None, "span", "line", None),
        check_vma=False,
    )
```

```python
import jax
import jax.numpy as jnp
from jax import lax
from jax.experimental import pallas as pl
from jax.experimental.pallas import tpu as pltpu
from jax.sharding import PartitionSpec as P

MESH = pl.DeviceIdType.MESH
f32 = jnp.float32
span_weight = 0.25
NV = 5
GROUP = 8
WIDE = 16
PACKS = 15
PAIRS = [(i, j) for i in range(NV) for j in range(i, NV)]
SYM = [[PAIRS.index((min(i, j), max(i, j))) for j in range(NV)] for i in range(NV)]
NSYM = len(PAIRS)


def roll(x, shift, axis):
    return pltpu.roll(x, shift, axis)


def mm(left, right):
    out = []
    for i in range(NV):
        acc = left[i][0][None] * right[0]
        for k in range(1, NV):
            acc = acc + left[i][k][None] * right[k]
        out.append(acc)
    return out


def inverse(m):
    m = [list(row) for row in m]
    for p in range(NV):
        r = 1.0 / m[p][p]
        for j in range(NV):
            if j != p:
                m[p][j] = m[p][j] * r
        for i in range(NV):
            if i != p:
                f = m[i][p]
                for j in range(NV):
                    if j != p:
                        m[i][j] = m[i][j] - f * m[p][j]
                m[i][p] = -(f * r)
        m[p][p] = r
    return m


def matvec(columns, v):
    acc = columns[0] * v[0][None]
    for k in range(1, NV):
        acc = acc + columns[k] * v[k][None]
    return acc


def tree_up_matrices(seg, la_ref, fb_ref, keep):
    def body(level, carry):
        back = GROUP - lax.shift_left(jnp.int32(1), level)
        fa = [seg[0, i] for i in range(NV)]
        la = [seg[1, i] for i in range(NV)]
        fb = [roll(x, back, 1) for x in fa]
        lb = [roll(x, back, 1) for x in la]
        t = mm([[la[i][NV + k] for k in range(NV)] for i in range(NV)], fb)
        eye = [[(1.0 if i == k else 0.0) - t[i][k] for k in range(NV)] for i in range(NV)]
        x = inverse(eye)
        q = [jnp.concatenate([la[i][0:NV], -t[i][NV:]], axis=0) for i in range(NV)]
        ela = mm(x, q)
        r = mm([[fb[i][k] for k in range(NV)] for i in range(NV)], ela)
        efb = [jnp.concatenate([-r[i][0:NV], fb[i][NV:] - r[i][NV:]], axis=0) for i in range(NV)]
        s = mm([[fa[i][NV + k] for k in range(NV)] for i in range(NV)], efb)
        y = mm([[lb[i][k] for k in range(NV)] for i in range(NV)], ela)
        for i in range(NV):
            for k in range(NV):
                keep[level, 0, k, i] = la[i][NV + k]
                keep[level, 1, k, i] = x[i][k]
                keep[level, 2, k, i] = fb[i][k]
                keep[level, 3, k, i] = fa[i][NV + k]
                keep[level, 4, k, i] = lb[i][k]
            la_ref[level, i, 0 : 2 * NV] = ela[i]
            fb_ref[level, i, 0 : 2 * NV] = efb[i]
            seg[0, i, 0:NV] = fa[i][0:NV] - s[i][0:NV]
            seg[0, i, NV:] = -s[i][NV:]
            seg[1, i, 0:NV] = -y[i][0:NV]
            seg[1, i, NV:] = lb[i][NV:] - y[i][NV:]
        return carry

    lax.fori_loop(0, 3, body, 0)


def tree_up_rhs(f, l, la_ref, fb_ref, keep):
    for level in range(3):
        back = GROUP - (1 << level)
        m = [[keep[level, w, k] for k in range(NV)] for w in range(5)]
        fb = roll(f, back, 1)
        lb = roll(l, back, 1)
        la_c = matvec(m[1], l - matvec(m[0], fb))
        fb_c = fb - matvec(m[2], la_c)
        f = f - matvec(m[3], fb_c)
        l = lb - matvec(m[4], la_c)
        for i in range(NV):
            la_ref[level, i, 2 * NV] = la_c[i]
            fb_ref[level, i, 2 * NV] = fb_c[i]
    return f, l


def spread(ref, index, column):
    return jnp.broadcast_to(
        ref[index + (column // 8, slice(column % 8, column % 8 + 1), slice(None))], (GROUP, 128)
    )


def tree_up_lanes(seg, near, temp, la_ref, fb_ref):
    tile = lax.broadcasted_iota(jnp.int32, (2, GROUP, 128), 0)
    column = tile * GROUP + lax.broadcasted_iota(jnp.int32, (2, GROUP, 128), 1)
    not_n = (column < NV) | (column == 2 * NV)
    not_p = column >= NV

    def body(level, carry):
        back = 128 - lax.shift_left(jnp.int32(WIDE), level)
        fa = [seg[0, i] for i in range(NV)]
        la = [seg[1, i] for i in range(NV)]
        fb = [roll(x, back, 2) for x in fa]
        lb = [roll(x, back, 2) for x in la]
        for i in range(NV):
            near[0, i] = fb[i]
            near[1, i] = lb[i]
        left = lambda ref, which, first: [
            [spread(ref, (which, i), first + k) for k in range(NV)] for i in range(NV)
        ]
        t = mm(left(seg, 1, NV), fb)
        for i in range(NV):
            temp[i] = t[i]
        eye = [
            [(1.0 if i == k else 0.0) - spread(temp, (i,), k) for k in range(NV)]
            for i in range(NV)
        ]
        x = inverse(eye)
        ela = mm(
            x, [jnp.where(not_n, la[i], 0.0) - jnp.where(not_p, t[i], 0.0) for i in range(NV)]
        )
        r = mm(left(near, 0, 0), ela)
        efb = [jnp.where(not_p, fb[i], 0.0) - r[i] for i in range(NV)]
        s = mm(left(seg, 0, NV), efb)
        y = mm(left(near, 1, 0), ela)
        for i in range(NV):
            la_ref[level, i] = ela[i]
            fb_ref[level, i] = efb[i]
            seg[0, i] = jnp.where(not_n, fa[i], 0.0) - s[i]
            seg[1, i] = jnp.where(not_p, lb[i], 0.0) - y[i]
        return carry

    lax.fori_loop(0, 3, body, 0)


def tree_down(p, n, la, fb, axis, base, pos):
    for level in (2, 1, 0):
        shift = base << level
        second = (pos & shift) != 0
        value = []
        for get in (la, fb):
            rows = []
            for i in range(NV):
                row = get(level, i, 2 * NV)
                if p is not None:
                    terms = [get(level, i, k) * p[k] for k in range(NV)]
                    terms += [get(level, i, NV + k) * n[k] for k in range(NV)]
                    while len(terms) > 1:
                        terms = [
                            terms[j] + terms[j + 1] if j + 1 < len(terms) else terms[j]
                            for j in range(0, len(terms), 2)
                        ]
                    row = row - terms[0]
                rows.append(row)
            value.append(rows)
        new_p = []
        new_n = []
        for i in range(NV):
            new_p.append(
                jnp.where(second, roll(value[0][i], shift, axis), 0.0 if p is None else p[i])
            )
            new_n.append(
                jnp.where(second, 0.0 if n is None else roll(n[i], shift, axis), value[1][i])
            )
        p, n = new_p, new_n
    return p, n


def swap_blocks(x):
    sub = lax.broadcasted_iota(jnp.int32, x.shape, 1)
    lane = lax.broadcasted_iota(jnp.int32, x.shape, 2)
    for bit in range(3):
        j = lax.shift_right_logical(sub, bit) & 1
        k = lax.shift_right_logical(lane, 4 + bit) & 1
        s = 1 << bit
        w = WIDE << bit
        up = roll(roll(x, GROUP - s, 1), w, 2)
        down = roll(roll(x, s, 1), 128 - w, 2)
        x = jnp.where(j == k, x, jnp.where(j == 0, up, down))
    return x


def kernel(
    jac_hbm, state_hbm, metric_hbm, diss_hbm, time_hbm, out_ref,
    jac_ref, state_ref, metric_ref, diss_ref, time_ref,
    sym_ref, flux_ref, fst, dst, xst, ls, us, fs,
    rim_out, rim_in, span_in,
    wc, pinv, hg, es,
    seg1, la1, fb1, keep, seg2, la2, fb2, seg3, la3, fb3, near, temp,
    tmp, a_out, a_in, b_out, b_in, c_out, c_in,
    load_sem, span_sem, rim_sem, a_sem, b_sem, c_sem,
):
    line = lax.axis_index("line")
    span = lax.axis_index("span")
    n_line = lax.axis_size("line")
    n_span = lax.axis_size("span")
    plane = line // GROUP
    member = line % GROUP
    line_next = lax.rem(line + 1, n_line)
    line_prev = lax.rem(line + n_line - 1, n_line)
    span_next = lax.rem(span + 1, n_span)
    span_prev = lax.rem(span + n_span - 1, n_span)
    members = [plane * GROUP + lax.rem(member + o, GROUP) for o in range(1, GROUP)]
    planes = [lax.rem(plane + o, GROUP) * GROUP + member for o in range(1, GROUP)]

    loads = [
        pltpu.make_async_copy(source, target, load_sem.at[i])
        for i, (source, target) in enumerate(
            (
                (jac_hbm, jac_ref),
                (state_hbm, state_ref),
                (metric_hbm, metric_ref),
                (diss_hbm, diss_ref),
                (time_hbm, time_ref),
            )
        )
    ]
    for c in loads:
        c.start()

    peers = [(line, span_next), (line, span_prev), (line_next, span), (line_prev, span)]
    peers += [(x, span) for x in members] + [(x, span) for x in planes]
    barrier = pltpu.get_barrier_semaphore()
    for peer in peers:
        pl.semaphore_signal(barrier, inc=1, device_id=peer, device_id_type=MESH)

    for c in loads:
        c.wait()
    metric = metric_ref[...]
    for q, (i, j) in enumerate(PAIRS):
        if i == j:
            value = jac_ref[i, i].astype(f32)
        else:
            value = 0.5 * (jac_ref[i, j].astype(f32) + jac_ref[j, i].astype(f32))
        sym_ref[q] = metric * value
    for i in range(NV):
        acc = sym_ref[SYM[i][0]] * state_ref[0]
        for k in range(1, NV):
            acc = acc + sym_ref[SYM[i][k]] * state_ref[k]
        flux_ref[i] = acc
    points = metric.shape[0]
    for side, row in ((0, points - 1), (1, 0)):
        for q in range(NSYM):
            rim_out[side, q : q + 1, :] = sym_ref[q, row : row + 1, :]
        for i in range(NV):
            rim_out[side, NSYM + i : NSYM + i + 1, :] = flux_ref[i, row : row + 1, :]
        rim_out[side, NSYM + NV : NSYM + NV + 1, :] = diss_ref[row : row + 1, :]
        rim_out[side, NSYM + NV + 1 :, :] = jnp.zeros((24 - NSYM - NV - 1, 128), f32)

    pl.semaphore_wait(barrier, len(peers))

    copies_rim = []
    for side, target in ((0, line_next), (1, line_prev)):
        copies_rim.append(
            pltpu.make_async_remote_copy(
                src_ref=rim_out.at[side], dst_ref=rim_in.at[side],
                send_sem=rim_sem.at[0, side], recv_sem=rim_sem.at[1, side],
                device_id=(target, span), device_id_type=MESH,
            )
        )
        copies_rim[-1].start()
    copies_span = []
    for side, target in ((0, span_next), (1, span_prev)):
        copies_span.append(
            pltpu.make_async_remote_copy(
                src_ref=state_hbm, dst_ref=span_in.at[side],
                send_sem=span_sem.at[0, side], recv_sem=span_sem.at[1, side],
                device_id=(line, target), device_id_type=MESH,
            )
        )
        copies_span[-1].start()

    for t in range(GROUP):
        fst[t + 1] = sym_ref[:, pl.ds(t, GROUP, stride=GROUP), :]
        xst[t + 1] = flux_ref[:, pl.ds(t, GROUP, stride=GROUP), :]
        dst[t + 1] = diss_ref[pl.ds(t, GROUP, stride=GROUP), :]
    def faces(t, carry):
        g = 0.25 * (fst[t] + fst[t + 1])
        f = 0.5 * (dst[t] + dst[t + 1])
        fs[t] = f
        for i in range(NV):
            for k in range(NV):
                e = g[SYM[i][k]]
                us[t, i, k] = e - f if i == k else e
                ls[t, i, k] = -e - f if i == k else -e
        return carry

    lax.fori_loop(1, GROUP, faces, 0)

    sub2 = lax.broadcasted_iota(jnp.int32, (GROUP, 128), 0)
    for c in copies_rim:
        c.wait()
    first_device = line == 0
    last_device = line == n_line - 1
    for side, at, source, turn, edge, outside in (
        (0, 0, GROUP, 1, 0, first_device),
        (1, GROUP + 1, 1, GROUP - 1, GROUP - 1, last_device),
    ):
        rim = jnp.where(outside, 0.0, rim_in[side])
        for q in range(NSYM):
            fst[at, q] = jnp.where(sub2 == edge, rim[q : q + 1, :], roll(fst[source, q], turn, 0))
        for i in range(NV):
            xst[at, i] = jnp.where(
                sub2 == edge, rim[NSYM + i : NSYM + i + 1, :], roll(xst[source, i], turn, 0)
            )
        dst[at] = jnp.where(
            sub2 == edge, rim[NSYM + NV : NSYM + NV + 1, :], roll(dst[source], turn, 0)
        )

    lax.fori_loop(0, 2, lambda t, carry: faces(t * GROUP, carry), 0)

    zero = jnp.zeros((GROUP, 128), f32)
    for i in range(NV):
        for k in range(2 * NV):
            wc[0, i, k] = zero - 1.0 if i == k else zero
    for t in range(GROUP):
        dst[t] = fs[t] + time_ref[pl.ds(t, GROUP, stride=GROUP), :] + fs[t + 1]

    def forward(t, carry):
        diag = dst[t]
        low = [[ls[t, i, k] for k in range(NV)] for i in range(NV)]
        prod = mm(low, [wc[t, i] for i in range(NV)])
        m = [
            [(diag - prod[i][NV + k]) if i == k else -prod[i][NV + k] for k in range(NV)]
            for i in range(NV)
        ]
        inv = inverse(m)
        for i in range(NV):
            for k in range(NV):
                pinv[t, k, i] = inv[i][k]
        w = mm(inv, [-prod[i][0:NV] for i in range(NV)])
        c = mm(inv, [us[t + 1, i] for i in range(NV)])
        for i in range(NV):
            wc[t + 1, i, 0:NV] = w[i]
            wc[t + 1, i, NV:] = c[i]
        return carry

    lax.fori_loop(0, GROUP, forward, 0)

    for i in range(NV):
        hg[GROUP - 1, i] = wc[GROUP, i]

    def spikes(step, carry):
        t = GROUP - 2 - step
        c = [[wc[t + 1, i, NV + k] for k in range(NV)] for i in range(NV)]
        prod = mm(c, [hg[t + 1, i] for i in range(NV)])
        for i in range(NV):
            hg[t, i, 0:NV] = wc[t + 1, i, 0:NV] - prod[i][0:NV]
            hg[t, i, NV:] = -prod[i][NV:]
        return carry

    lax.fori_loop(0, GROUP - 1, spikes, 0)

    for which, t in ((0, 0), (1, GROUP - 1)):
        for i in range(NV):
            seg1[which, i] = hg[t, i]
    tree_up_matrices(seg1, la1, fb1, keep)

    def slot(which, i, column):
        if column < 8:
            return which * NV + i, column
        return 2 * NV + i, which * 3 + column - 8

    for i in range(NV):
        tmp[2 * NV + i, 6:8, :] = jnp.zeros((2, 128), f32)
    for which in range(2):
        for i in range(NV):
            for c in range(2 * NV):
                r, j = slot(which, i, c)
                tmp[r, j : j + 1, :] = seg1[which, i, c, 0:1, :]

    for c in copies_span:
        c.wait()
    no_prev = span == 0
    no_next = span == n_span - 1
    d = jnp.zeros((NV, GROUP, 128), f32)
    for t in range(GROUP):
        rows = pl.ds(t, GROUP, stride=GROUP)
        before = jnp.where(no_prev, 0.0, span_in[0, :, rows, :])
        after = jnp.where(no_next, 0.0, span_in[1, :, rows, :])
        rhs = -0.5 * (xst[t + 2] - xst[t])
        rhs = rhs + span_weight * (after - 2.0 * state_ref[:, rows, :] + before)
        for k in range(NV):
            rhs = rhs - ls[t, k] * d[k][None]
        d = pinv[t, 0] * rhs[0][None]
        for k in range(1, NV):
            d = d + pinv[t, k] * rhs[k][None]
        es[t] = d
    e = d
    for t in range(GROUP - 2, -1, -1):
        rows = [
            es[t, i] - jnp.sum(wc[t + 1, i, NV:] * e, axis=0) for i in range(NV)
        ]
        for i in range(NV):
            es[t, i] = rows[i]
        e = es[t]

    first, last = tree_up_rhs(es[0], es[GROUP - 1], la1, fb1, keep)

    def two_port_load(seg, landed):
        for s in range(GROUP):
            for r in range(PACKS):
                tmp[r, s : s + 1, :] = landed[s, r]
        packed = swap_blocks(tmp[...])
        for i in range(NV):
            seg[0, i, 0] = packed[i]
            seg[1, i, 0] = packed[NV + i]
            seg[0, i, 1] = packed[2 * NV + i]
            seg[1, i, 1] = roll(packed[2 * NV + i], GROUP - 3, 0)

    for which, value in ((0, first), (1, last)):
        for i in range(NV):
            r, j = slot(which, i, 2 * NV)
            tmp[r, j : j + 1, :] = value[i, 0:1, :]
    packed = swap_blocks(tmp[...])
    for s in range(GROUP):
        for r in range(PACKS):
            a_out[s, r] = packed[r, s : s + 1, :]
    copies = []
    for o in range(1, GROUP):
        copies.append(
            pltpu.make_async_remote_copy(
                src_ref=a_out.at[lax.rem(member + o, GROUP)], dst_ref=a_in.at[member],
                send_sem=a_sem.at[0, o], recv_sem=a_sem.at[1, o],
                device_id=(members[o - 1], span), device_id_type=MESH,
            )
        )
        copies[-1].start()
    a_in[member] = a_out[member]
    for c in copies:
        c.wait()
    two_port_load(seg2, a_in)
    tree_up_lanes(seg2, near, temp, la2, fb2)

    packed = swap_blocks(
        jnp.concatenate(
            [seg2[0, :, 0], seg2[1, :, 0]]
            + [
                jnp.where(sub2 < 3, seg2[0, i, 1], roll(seg2[1, i, 1], 3, 0))[None]
                for i in range(NV)
            ],
            axis=0,
        )
    )
    for r in range(PACKS):
        b_out[r] = packed[r, 0:1, :]
    copies = []
    for o in range(1, GROUP):
        copies.append(
            pltpu.make_async_remote_copy(
                src_ref=b_out, dst_ref=b_in.at[plane],
                send_sem=b_sem.at[0, o], recv_sem=b_sem.at[1, o],
                device_id=(planes[o - 1], span), device_id_type=MESH,
            )
        )
        copies[-1].start()
    b_in[plane] = b_out[...]
    for c in copies:
        c.wait()
    two_port_load(seg3, b_in)
    tree_up_lanes(seg3, near, temp, la3, fb3)

    lane = lax.broadcasted_iota(jnp.int32, (GROUP, 128), 1)
    get = lambda ref: lambda level, i, column: spread(ref, (level, i), column)
    p, n = tree_down(None, None, get(la3), get(fb3), 1, WIDE, lane)
    own = lax.rem(128 - plane * WIDE, 128)
    p = [roll(x, own, 1) for x in p]
    n = [roll(x, own, 1) for x in n]
    p, n = tree_down(p, n, get(la2), get(fb2), 1, WIDE, lane)

    for r, values in ((0, p), (1, n)):
        tile = values[0]
        for i in range(1, NV):
            tile = jnp.where(sub2 == i, values[i], tile)
        tmp[r] = tile
    packed = swap_blocks(tmp[0:2])
    for s in range(GROUP):
        for r in range(2):
            c_out[s, r] = packed[r, s : s + 1, :]
    copies = []
    for o in range(1, GROUP):
        copies.append(
            pltpu.make_async_remote_copy(
                src_ref=c_out.at[lax.rem(member + o, GROUP)], dst_ref=c_in.at[member],
                send_sem=c_sem.at[0, o], recv_sem=c_sem.at[1, o],
                device_id=(members[o - 1], span), device_id_type=MESH,
            )
        )
        copies[-1].start()
    c_in[member] = c_out[member]
    for c in copies:
        c.wait()
    for s in range(GROUP):
        for r in range(2):
            tmp[r, s : s + 1, :] = c_in[s, r]
    packed = swap_blocks(tmp[0:2])
    p = [jnp.broadcast_to(packed[0, i : i + 1, :], (GROUP, 128)) for i in range(NV)]
    n = [jnp.broadcast_to(packed[1, i : i + 1, :], (GROUP, 128)) for i in range(NV)]
    get = lambda ref: lambda level, i, column: ref[level, i, column]
    p, n = tree_down(p, n, get(la1), get(fb1), 0, 1, sub2)
    pn = jnp.concatenate([x[None] for x in p + n], axis=0)
    for t in range(GROUP):
        for i in range(NV):
            out_ref[i, pl.ds(t, GROUP, stride=GROUP), :] = es[t, i] - jnp.sum(
                hg[t, i] * pn, axis=0
            )


def per_device(jacobian, state, metric, dissipation, time_term):
    nv = state.shape[0]
    points, lines = metric.shape[1:]
    vmem = pl.BlockSpec(memory_space=pltpu.VMEM)
    tile = (GROUP, lines)

    update = pl.pallas_call(
        kernel,
        out_shape=jax.ShapeDtypeStruct((nv, points, lines), f32),
        in_specs=[pl.BlockSpec(memory_space=pl.ANY)] * 5,
        out_specs=vmem,
        scratch_shapes=[
            pltpu.VMEM((nv, nv, points, lines), jacobian.dtype),
            pltpu.VMEM((nv, points, lines), f32),
            pltpu.VMEM((points, lines), f32),
            pltpu.VMEM((points, lines), f32),
            pltpu.VMEM((points, lines), f32),
            pltpu.VMEM((NSYM, points, lines), f32),
            pltpu.VMEM((nv, points, lines), f32),
            pltpu.VMEM((GROUP + 2, NSYM) + tile, f32),
            pltpu.VMEM((GROUP + 2,) + tile, f32),
            pltpu.VMEM((GROUP + 2, nv) + tile, f32),
            pltpu.VMEM((GROUP + 1, nv, nv) + tile, f32),
            pltpu.VMEM((GROUP + 1, nv, nv) + tile, f32),
            pltpu.VMEM((GROUP + 1,) + tile, f32),
            pltpu.VMEM((2, 24, lines), f32),
            pltpu.VMEM((2, 24, lines), f32),
            pltpu.VMEM((2, nv, points, lines), f32),
            pltpu.VMEM((GROUP + 1, nv, 2 * nv) + tile, f32),
            pltpu.VMEM((GROUP, nv, nv) + tile, f32),
            pltpu.VMEM((GROUP, nv, 2 * nv) + tile, f32),
            pltpu.VMEM((GROUP, nv) + tile, f32),
            pltpu.VMEM((2, nv, 2 * nv) + tile, f32),
            pltpu.VMEM((3, nv, 2 * nv + 1) + tile, f32),
            pltpu.VMEM((3, nv, 2 * nv + 1) + tile, f32),
            pltpu.VMEM((3, 5, nv, nv) + tile, f32),
            pltpu.VMEM((2, nv, 2) + tile, f32),
            pltpu.VMEM((3, nv, 2) + tile, f32),
            pltpu.VMEM((3, nv, 2) + tile, f32),
            pltpu.VMEM((2, nv, 2) + tile, f32),
            pltpu.VMEM((3, nv, 2) + tile, f32),
            pltpu.VMEM((3, nv, 2) + tile, f32),
            pltpu.VMEM((2, nv, 2) + tile, f32),
            pltpu.VMEM((nv, 2) + tile, f32),
            pltpu.VMEM((PACKS,) + tile, f32),
            pltpu.VMEM((GROUP, PACKS, 1, lines), f32),
            pltpu.VMEM((GROUP, PACKS, 1, lines), f32),
            pltpu.VMEM((PACKS, 1, lines), f32),
            pltpu.VMEM((GROUP, PACKS, 1, lines), f32),
            pltpu.VMEM((GROUP, 2, 1, lines), f32),
            pltpu.VMEM((GROUP, 2, 1, lines), f32),
            pltpu.SemaphoreType.DMA((5,)),
            pltpu.SemaphoreType.DMA((2, 2)),
            pltpu.SemaphoreType.DMA((2, 2)),
            pltpu.SemaphoreType.DMA((2, GROUP)),
            pltpu.SemaphoreType.DMA((2, GROUP)),
            pltpu.SemaphoreType.DMA((2, GROUP)),
        ],
        compiler_params=pltpu.CompilerParams(collective_id=0, has_side_effects=True),
        name="sweep",
    )(
        jacobian.reshape((nv, nv, points, lines)),
        state.reshape((nv, points, lines)),
        metric.reshape((points, lines)),
        dissipation.reshape((points, lines)),
        time_term.reshape((points, lines)),
    )
    return update.reshape(state.shape)


def solution(mesh):
    return jax.shard_map(
        per_device,
        mesh=mesh,
        in_specs=(
            P(None, None, "span", "line", None),
            P(None, "span", "line", None),
            P("span", "line", None),
            P("span", "line", None),
            P("span", "line", None),
        ),
        out_specs=P(None, "span", "line", None),
        check_vma=False,
    )
```

```python
import jax
import jax.numpy as jnp
from jax import lax
from jax.experimental import pallas as pl
from jax.experimental.pallas import tpu as pltpu
from jax.sharding import PartitionSpec as P

MESH = pl.DeviceIdType.MESH
f32 = jnp.float32
span_weight = 0.25
NV = 5
GROUP = 8
WIDE = 16
PACKS = 15
PAIRS = [(i, j) for i in range(NV) for j in range(i, NV)]
SYM = [[PAIRS.index((min(i, j), max(i, j))) for j in range(NV)] for i in range(NV)]
NSYM = len(PAIRS)


def roll(x, shift, axis):
    return pltpu.roll(x, shift, axis)


def mm(left, right):
    out = []
    for i in range(NV):
        acc = left[i][0][None] * right[0]
        for k in range(1, NV):
            acc = acc + left[i][k][None] * right[k]
        out.append(acc)
    return out


def inverse(m):
    m = [list(row) for row in m]
    for p in range(NV):
        r = 1.0 / m[p][p]
        for j in range(NV):
            if j != p:
                m[p][j] = m[p][j] * r
        for i in range(NV):
            if i != p:
                f = m[i][p]
                for j in range(NV):
                    if j != p:
                        m[i][j] = m[i][j] - f * m[p][j]
                m[i][p] = -(f * r)
        m[p][p] = r
    return m


def matvec(columns, v):
    acc = columns[0] * v[0][None]
    for k in range(1, NV):
        acc = acc + columns[k] * v[k][None]
    return acc


def tree_up_matrices(seg, la_ref, fb_ref, keep):
    def body(level, carry):
        back = GROUP - lax.shift_left(jnp.int32(1), level)
        fa = [seg[0, i] for i in range(NV)]
        la = [seg[1, i] for i in range(NV)]
        fb = [roll(x, back, 1) for x in fa]
        lb = [roll(x, back, 1) for x in la]
        t = mm([[la[i][NV + k] for k in range(NV)] for i in range(NV)], fb)
        eye = [[(1.0 if i == k else 0.0) - t[i][k] for k in range(NV)] for i in range(NV)]
        x = inverse(eye)
        q = [jnp.concatenate([la[i][0:NV], -t[i][NV:]], axis=0) for i in range(NV)]
        ela = mm(x, q)
        r = mm([[fb[i][k] for k in range(NV)] for i in range(NV)], ela)
        efb = [jnp.concatenate([-r[i][0:NV], fb[i][NV:] - r[i][NV:]], axis=0) for i in range(NV)]
        s = mm([[fa[i][NV + k] for k in range(NV)] for i in range(NV)], efb)
        y = mm([[lb[i][k] for k in range(NV)] for i in range(NV)], ela)
        for i in range(NV):
            for k in range(NV):
                keep[level, 0, k, i] = la[i][NV + k]
                keep[level, 1, k, i] = x[i][k]
                keep[level, 2, k, i] = fb[i][k]
                keep[level, 3, k, i] = fa[i][NV + k]
                keep[level, 4, k, i] = lb[i][k]
            la_ref[level, i, 0 : 2 * NV] = ela[i]
            fb_ref[level, i, 0 : 2 * NV] = efb[i]
            seg[0, i, 0:NV] = fa[i][0:NV] - s[i][0:NV]
            seg[0, i, NV:] = -s[i][NV:]
            seg[1, i, 0:NV] = -y[i][0:NV]
            seg[1, i, NV:] = lb[i][NV:] - y[i][NV:]
        return carry

    lax.fori_loop(0, 3, body, 0)


def tree_up_rhs(f, l, la_ref, fb_ref, keep):
    for level in range(3):
        back = GROUP - (1 << level)
        m = [[keep[level, w, k] for k in range(NV)] for w in range(5)]
        fb = roll(f, back, 1)
        lb = roll(l, back, 1)
        la_c = matvec(m[1], l - matvec(m[0], fb))
        fb_c = fb - matvec(m[2], la_c)
        f = f - matvec(m[3], fb_c)
        l = lb - matvec(m[4], la_c)
        for i in range(NV):
            la_ref[level, i, 2 * NV] = la_c[i]
            fb_ref[level, i, 2 * NV] = fb_c[i]
    return f, l


def spread(ref, index, column):
    return jnp.broadcast_to(
        ref[index + (column // 8, slice(column % 8, column % 8 + 1), slice(None))], (GROUP, 128)
    )


def tree_up_lanes(seg, near, temp, la_ref, fb_ref):
    tile = lax.broadcasted_iota(jnp.int32, (2, GROUP, 128), 0)
    column = tile * GROUP + lax.broadcasted_iota(jnp.int32, (2, GROUP, 128), 1)
    not_n = (column < NV) | (column == 2 * NV)
    not_p = column >= NV

    def body(level, carry):
        back = 128 - lax.shift_left(jnp.int32(WIDE), level)
        fa = [seg[0, i] for i in range(NV)]
        la = [seg[1, i] for i in range(NV)]
        fb = [roll(x, back, 2) for x in fa]
        lb = [roll(x, back, 2) for x in la]
        for i in range(NV):
            near[0, i] = fb[i]
            near[1, i] = lb[i]
        left = lambda ref, which, first: [
            [spread(ref, (which, i), first + k) for k in range(NV)] for i in range(NV)
        ]
        t = mm(left(seg, 1, NV), fb)
        for i in range(NV):
            temp[i] = t[i]
        eye = [
            [(1.0 if i == k else 0.0) - spread(temp, (i,), k) for k in range(NV)]
            for i in range(NV)
        ]
        x = inverse(eye)
        ela = mm(
            x, [jnp.where(not_n, la[i], 0.0) - jnp.where(not_p, t[i], 0.0) for i in range(NV)]
        )
        r = mm(left(near, 0, 0), ela)
        efb = [jnp.where(not_p, fb[i], 0.0) - r[i] for i in range(NV)]
        s = mm(left(seg, 0, NV), efb)
        y = mm(left(near, 1, 0), ela)
        for i in range(NV):
            la_ref[level, i] = ela[i]
            fb_ref[level, i] = efb[i]
            seg[0, i] = jnp.where(not_n, fa[i], 0.0) - s[i]
            seg[1, i] = jnp.where(not_p, lb[i], 0.0) - y[i]
        return carry

    lax.fori_loop(0, 3, body, 0)


def tree_down(p, n, la, fb, axis, base, pos):
    for level in (2, 1, 0):
        shift = base << level
        second = (pos & shift) != 0
        value = []
        for get in (la, fb):
            rows = []
            for i in range(NV):
                row = get(level, i, 2 * NV)
                if p is not None:
                    terms = [get(level, i, k) * p[k] for k in range(NV)]
                    terms += [get(level, i, NV + k) * n[k] for k in range(NV)]
                    while len(terms) > 1:
                        terms = [
                            terms[j] + terms[j + 1] if j + 1 < len(terms) else terms[j]
                            for j in range(0, len(terms), 2)
                        ]
                    row = row - terms[0]
                rows.append(row)
            value.append(rows)
        new_p = []
        new_n = []
        for i in range(NV):
            new_p.append(
                jnp.where(second, roll(value[0][i], shift, axis), 0.0 if p is None else p[i])
            )
            new_n.append(
                jnp.where(second, 0.0 if n is None else roll(n[i], shift, axis), value[1][i])
            )
        p, n = new_p, new_n
    return p, n


def swap_blocks(x):
    sub = lax.broadcasted_iota(jnp.int32, x.shape, 1)
    lane = lax.broadcasted_iota(jnp.int32, x.shape, 2)
    for bit in range(3):
        j = lax.shift_right_logical(sub, bit) & 1
        k = lax.shift_right_logical(lane, 4 + bit) & 1
        s = 1 << bit
        w = WIDE << bit
        up = roll(roll(x, GROUP - s, 1), w, 2)
        down = roll(roll(x, s, 1), 128 - w, 2)
        x = jnp.where(j == k, x, jnp.where(j == 0, up, down))
    return x


def kernel(
    jac_hbm, state_hbm, metric_hbm, diss_hbm, time_hbm, out_ref,
    jac_ref, state_ref, metric_ref, diss_ref, time_ref,
    sym_ref, flux_ref, fst, dst, xst, ls, us, fs,
    rim_out, rim_in, span_in,
    wc, pinv, hg, es,
    seg1, la1, fb1, keep, seg2, la2, fb2, seg3, la3, fb3, near, temp,
    tmp, a_out, a_in, b_out, b_in, c_out, c_in,
    line_sem, plane_sem, load_sem, span_sem, rim_sem, a_sem, b_sem, c_sem,
):
    line = lax.axis_index("line")
    span = lax.axis_index("span")
    n_line = lax.axis_size("line")
    n_span = lax.axis_size("span")
    plane = line // GROUP
    member = line % GROUP
    line_next = lax.rem(line + 1, n_line)
    line_prev = lax.rem(line + n_line - 1, n_line)
    span_next = lax.rem(span + 1, n_span)
    span_prev = lax.rem(span + n_span - 1, n_span)
    far_first = sorted(range(1, GROUP), key=lambda o: abs(o - GROUP // 2))
    members = [plane * GROUP + lax.rem(member + o, GROUP) for o in range(1, GROUP)]
    planes = [lax.rem(plane + o, GROUP) * GROUP + member for o in range(1, GROUP)]

    loads = [
        pltpu.make_async_copy(source, target, load_sem.at[i])
        for i, (source, target) in enumerate(
            (
                (jac_hbm, jac_ref),
                (state_hbm, state_ref),
                (metric_hbm, metric_ref),
                (diss_hbm, diss_ref),
                (time_hbm, time_ref),
            )
        )
    ]
    for c in loads:
        c.start()

    peers = [(line, span_next), (line, span_prev), (line_next, span), (line_prev, span)]
    peers += [(planes[0], span), (planes[-1], span)]
    barrier = pltpu.get_barrier_semaphore()
    for peer in peers:
        pl.semaphore_signal(barrier, inc=1, device_id=peer, device_id_type=MESH)

    for c in loads:
        c.wait()
    metric = metric_ref[...]
    for q, (i, j) in enumerate(PAIRS):
        if i == j:
            value = jac_ref[i, i].astype(f32)
        else:
            value = 0.5 * (jac_ref[i, j].astype(f32) + jac_ref[j, i].astype(f32))
        sym_ref[q] = metric * value
    for i in range(NV):
        acc = sym_ref[SYM[i][0]] * state_ref[0]
        for k in range(1, NV):
            acc = acc + sym_ref[SYM[i][k]] * state_ref[k]
        flux_ref[i] = acc
    points = metric.shape[0]
    for side, row in ((0, points - 1), (1, 0)):
        for q in range(NSYM):
            rim_out[side, q : q + 1, :] = sym_ref[q, row : row + 1, :]
        for i in range(NV):
            rim_out[side, NSYM + i : NSYM + i + 1, :] = flux_ref[i, row : row + 1, :]
        rim_out[side, NSYM + NV : NSYM + NV + 1, :] = diss_ref[row : row + 1, :]
        rim_out[side, NSYM + NV + 1 :, :] = jnp.zeros((24 - NSYM - NV - 1, 128), f32)

    pl.semaphore_wait(barrier, len(peers))

    def greet(sem, size, step, position, spread_by, round_at):
        reach = (1 << round_at)
        for other in (lax.rem(position + reach, size), lax.rem(position + size - reach, size)):
            pl.semaphore_signal(
                sem.at[round_at], inc=1, device_id=(other * step + spread_by, span),
                device_id_type=MESH,
            )

    def greet_line(round_at):
        greet(line_sem, n_line, 1, line, 0, round_at)

    def greet_plane(round_at):
        greet(plane_sem, n_line // GROUP, GROUP, plane, member, round_at)

    greet_line(0)
    greet_plane(0)

    copies_rim = []
    for side, target in ((0, line_next), (1, line_prev)):
        copies_rim.append(
            pltpu.make_async_remote_copy(
                src_ref=rim_out.at[side], dst_ref=rim_in.at[side],
                send_sem=rim_sem.at[0, side], recv_sem=rim_sem.at[1, side],
                device_id=(target, span), device_id_type=MESH,
            )
        )
        copies_rim[-1].start()
    copies_span = []
    for side, target in ((0, span_next), (1, span_prev)):
        copies_span.append(
            pltpu.make_async_remote_copy(
                src_ref=state_hbm, dst_ref=span_in.at[side],
                send_sem=span_sem.at[0, side], recv_sem=span_sem.at[1, side],
                device_id=(line, target), device_id_type=MESH,
            )
        )
        copies_span[-1].start()

    for t in range(GROUP):
        fst[t + 1] = sym_ref[:, pl.ds(t, GROUP, stride=GROUP), :]
        xst[t + 1] = flux_ref[:, pl.ds(t, GROUP, stride=GROUP), :]
        dst[t + 1] = diss_ref[pl.ds(t, GROUP, stride=GROUP), :]
    def faces(t, carry):
        g = 0.25 * (fst[t] + fst[t + 1])
        f = 0.5 * (dst[t] + dst[t + 1])
        fs[t] = f
        for i in range(NV):
            for k in range(NV):
                e = g[SYM[i][k]]
                us[t, i, k] = e - f if i == k else e
                ls[t, i, k] = -e - f if i == k else -e
        return carry

    lax.fori_loop(1, GROUP, faces, 0)

    sub2 = lax.broadcasted_iota(jnp.int32, (GROUP, 128), 0)
    for c in copies_rim:
        c.wait()
    first_device = line == 0
    last_device = line == n_line - 1
    for side, at, source, turn, edge, outside in (
        (0, 0, GROUP, 1, 0, first_device),
        (1, GROUP + 1, 1, GROUP - 1, GROUP - 1, last_device),
    ):
        rim = jnp.where(outside, 0.0, rim_in[side])
        for q in range(NSYM):
            fst[at, q] = jnp.where(sub2 == edge, rim[q : q + 1, :], roll(fst[source, q], turn, 0))
        for i in range(NV):
            xst[at, i] = jnp.where(
                sub2 == edge, rim[NSYM + i : NSYM + i + 1, :], roll(xst[source, i], turn, 0)
            )
        dst[at] = jnp.where(
            sub2 == edge, rim[NSYM + NV : NSYM + NV + 1, :], roll(dst[source], turn, 0)
        )

    lax.fori_loop(0, 2, lambda t, carry: faces(t * GROUP, carry), 0)

    zero = jnp.zeros((GROUP, 128), f32)
    for i in range(NV):
        for k in range(2 * NV):
            wc[0, i, k] = zero - 1.0 if i == k else zero
    for t in range(GROUP):
        dst[t] = fs[t] + time_ref[pl.ds(t, GROUP, stride=GROUP), :] + fs[t + 1]

    def forward(t, carry):
        diag = dst[t]
        low = [[ls[t, i, k] for k in range(NV)] for i in range(NV)]
        prod = mm(low, [wc[t, i] for i in range(NV)])
        m = [
            [(diag - prod[i][NV + k]) if i == k else -prod[i][NV + k] for k in range(NV)]
            for i in range(NV)
        ]
        inv = inverse(m)
        for i in range(NV):
            for k in range(NV):
                pinv[t, k, i] = inv[i][k]
        w = mm(inv, [-prod[i][0:NV] for i in range(NV)])
        c = mm(inv, [us[t + 1, i] for i in range(NV)])
        for i in range(NV):
            wc[t + 1, i, 0:NV] = w[i]
            wc[t + 1, i, NV:] = c[i]
        return carry

    lax.fori_loop(0, GROUP, forward, 0)
    pl.semaphore_wait(line_sem.at[0], 2)
    pl.semaphore_wait(plane_sem.at[0], 2)
    greet_line(1)
    greet_plane(1)

    for i in range(NV):
        hg[GROUP - 1, i] = wc[GROUP, i]

    def spikes(step, carry):
        t = GROUP - 2 - step
        c = [[wc[t + 1, i, NV + k] for k in range(NV)] for i in range(NV)]
        prod = mm(c, [hg[t + 1, i] for i in range(NV)])
        for i in range(NV):
            hg[t, i, 0:NV] = wc[t + 1, i, 0:NV] - prod[i][0:NV]
            hg[t, i, NV:] = -prod[i][NV:]
        return carry

    lax.fori_loop(0, GROUP - 1, spikes, 0)
    pl.semaphore_wait(line_sem.at[1], 2)
    greet_line(2)

    for which, t in ((0, 0), (1, GROUP - 1)):
        for i in range(NV):
            seg1[which, i] = hg[t, i]
    tree_up_matrices(seg1, la1, fb1, keep)

    def slot(which, i, column):
        if column < 8:
            return which * NV + i, column
        return 2 * NV + i, which * 3 + column - 8

    for i in range(NV):
        tmp[2 * NV + i, 6:8, :] = jnp.zeros((2, 128), f32)
    for which in range(2):
        for i in range(NV):
            for c in range(2 * NV):
                r, j = slot(which, i, c)
                tmp[r, j : j + 1, :] = seg1[which, i, c, 0:1, :]

    pl.semaphore_wait(line_sem.at[2], 2)
    pl.semaphore_wait(plane_sem.at[1], 2)
    for c in copies_span:
        c.wait()
    no_prev = span == 0
    no_next = span == n_span - 1
    d = jnp.zeros((NV, GROUP, 128), f32)
    for t in range(GROUP):
        rows = pl.ds(t, GROUP, stride=GROUP)
        before = jnp.where(no_prev, 0.0, span_in[0, :, rows, :])
        after = jnp.where(no_next, 0.0, span_in[1, :, rows, :])
        rhs = -0.5 * (xst[t + 2] - xst[t])
        rhs = rhs + span_weight * (after - 2.0 * state_ref[:, rows, :] + before)
        for k in range(NV):
            rhs = rhs - ls[t, k] * d[k][None]
        d = pinv[t, 0] * rhs[0][None]
        for k in range(1, NV):
            d = d + pinv[t, k] * rhs[k][None]
        es[t] = d
    e = d
    for t in range(GROUP - 2, -1, -1):
        rows = [
            es[t, i] - jnp.sum(wc[t + 1, i, NV:] * e, axis=0) for i in range(NV)
        ]
        for i in range(NV):
            es[t, i] = rows[i]
        e = es[t]

    first, last = tree_up_rhs(es[0], es[GROUP - 1], la1, fb1, keep)

    def two_port_load(seg, landed):
        for s in range(GROUP):
            for r in range(PACKS):
                tmp[r, s : s + 1, :] = landed[s, r]
        packed = swap_blocks(tmp[...])
        for i in range(NV):
            seg[0, i, 0] = packed[i]
            seg[1, i, 0] = packed[NV + i]
            seg[0, i, 1] = packed[2 * NV + i]
            seg[1, i, 1] = roll(packed[2 * NV + i], GROUP - 3, 0)

    for which, value in ((0, first), (1, last)):
        for i in range(NV):
            r, j = slot(which, i, 2 * NV)
            tmp[r, j : j + 1, :] = value[i, 0:1, :]
    packed = swap_blocks(tmp[...])
    for s in range(GROUP):
        for r in range(PACKS):
            a_out[s, r] = packed[r, s : s + 1, :]
    copies = []
    for o in far_first:
        copies.append(
            pltpu.make_async_remote_copy(
                src_ref=a_out.at[lax.rem(member + o, GROUP)], dst_ref=a_in.at[member],
                send_sem=a_sem.at[0, o], recv_sem=a_sem.at[1, o],
                device_id=(members[o - 1], span), device_id_type=MESH,
            )
        )
        copies[-1].start()
    a_in[member] = a_out[member]
    for c in copies:
        c.wait()
    two_port_load(seg2, a_in)
    tree_up_lanes(seg2, near, temp, la2, fb2)

    packed = swap_blocks(
        jnp.concatenate(
            [seg2[0, :, 0], seg2[1, :, 0]]
            + [
                jnp.where(sub2 < 3, seg2[0, i, 1], roll(seg2[1, i, 1], 3, 0))[None]
                for i in range(NV)
            ],
            axis=0,
        )
    )
    for r in range(PACKS):
        b_out[r] = packed[r, 0:1, :]
    copies = []
    for o in far_first:
        copies.append(
            pltpu.make_async_remote_copy(
                src_ref=b_out, dst_ref=b_in.at[plane],
                send_sem=b_sem.at[0, o], recv_sem=b_sem.at[1, o],
                device_id=(planes[o - 1], span), device_id_type=MESH,
            )
        )
        copies[-1].start()
    b_in[plane] = b_out[...]
    for c in copies:
        c.wait()
    two_port_load(seg3, b_in)
    tree_up_lanes(seg3, near, temp, la3, fb3)

    lane = lax.broadcasted_iota(jnp.int32, (GROUP, 128), 1)
    get = lambda ref: lambda level, i, column: spread(ref, (level, i), column)
    p, n = tree_down(None, None, get(la3), get(fb3), 1, WIDE, lane)
    own = lax.rem(128 - plane * WIDE, 128)
    p = [roll(x, own, 1) for x in p]
    n = [roll(x, own, 1) for x in n]
    p, n = tree_down(p, n, get(la2), get(fb2), 1, WIDE, lane)

    for r, values in ((0, p), (1, n)):
        tile = values[0]
        for i in range(1, NV):
            tile = jnp.where(sub2 == i, values[i], tile)
        tmp[r] = tile
    packed = swap_blocks(tmp[0:2])
    for s in range(GROUP):
        for r in range(2):
            c_out[s, r] = packed[r, s : s + 1, :]
    copies = []
    for o in far_first:
        copies.append(
            pltpu.make_async_remote_copy(
                src_ref=c_out.at[lax.rem(member + o, GROUP)], dst_ref=c_in.at[member],
                send_sem=c_sem.at[0, o], recv_sem=c_sem.at[1, o],
                device_id=(members[o - 1], span), device_id_type=MESH,
            )
        )
        copies[-1].start()
    c_in[member] = c_out[member]
    for c in copies:
        c.wait()
    for s in range(GROUP):
        for r in range(2):
            tmp[r, s : s + 1, :] = c_in[s, r]
    packed = swap_blocks(tmp[0:2])
    p = [jnp.broadcast_to(packed[0, i : i + 1, :], (GROUP, 128)) for i in range(NV)]
    n = [jnp.broadcast_to(packed[1, i : i + 1, :], (GROUP, 128)) for i in range(NV)]
    get = lambda ref: lambda level, i, column: ref[level, i, column]
    p, n = tree_down(p, n, get(la1), get(fb1), 0, 1, sub2)
    pn = jnp.concatenate([x[None] for x in p + n], axis=0)
    for t in range(GROUP):
        for i in range(NV):
            out_ref[i, pl.ds(t, GROUP, stride=GROUP), :] = es[t, i] - jnp.sum(
                hg[t, i] * pn, axis=0
            )


def per_device(jacobian, state, metric, dissipation, time_term):
    nv = state.shape[0]
    points, lines = metric.shape[1:]
    vmem = pl.BlockSpec(memory_space=pltpu.VMEM)
    tile = (GROUP, lines)

    update = pl.pallas_call(
        kernel,
        out_shape=pltpu.VMEM((nv, points, lines), f32),
        in_specs=[pl.BlockSpec(memory_space=pl.ANY)] * 5,
        out_specs=vmem,
        scratch_shapes=[
            pltpu.VMEM((nv, nv, points, lines), jacobian.dtype),
            pltpu.VMEM((nv, points, lines), f32),
            pltpu.VMEM((points, lines), f32),
            pltpu.VMEM((points, lines), f32),
            pltpu.VMEM((points, lines), f32),
            pltpu.VMEM((NSYM, points, lines), f32),
            pltpu.VMEM((nv, points, lines), f32),
            pltpu.VMEM((GROUP + 2, NSYM) + tile, f32),
            pltpu.VMEM((GROUP + 2,) + tile, f32),
            pltpu.VMEM((GROUP + 2, nv) + tile, f32),
            pltpu.VMEM((GROUP + 1, nv, nv) + tile, f32),
            pltpu.VMEM((GROUP + 1, nv, nv) + tile, f32),
            pltpu.VMEM((GROUP + 1,) + tile, f32),
            pltpu.VMEM((2, 24, lines), f32),
            pltpu.VMEM((2, 24, lines), f32),
            pltpu.VMEM((2, nv, points, lines), f32),
            pltpu.VMEM((GROUP + 1, nv, 2 * nv) + tile, f32),
            pltpu.VMEM((GROUP, nv, nv) + tile, f32),
            pltpu.VMEM((GROUP, nv, 2 * nv) + tile, f32),
            pltpu.VMEM((GROUP, nv) + tile, f32),
            pltpu.VMEM((2, nv, 2 * nv) + tile, f32),
            pltpu.VMEM((3, nv, 2 * nv + 1) + tile, f32),
            pltpu.VMEM((3, nv, 2 * nv + 1) + tile, f32),
            pltpu.VMEM((3, 5, nv, nv) + tile, f32),
            pltpu.VMEM((2, nv, 2) + tile, f32),
            pltpu.VMEM((3, nv, 2) + tile, f32),
            pltpu.VMEM((3, nv, 2) + tile, f32),
            pltpu.VMEM((2, nv, 2) + tile, f32),
            pltpu.VMEM((3, nv, 2) + tile, f32),
            pltpu.VMEM((3, nv, 2) + tile, f32),
            pltpu.VMEM((2, nv, 2) + tile, f32),
            pltpu.VMEM((nv, 2) + tile, f32),
            pltpu.VMEM((PACKS,) + tile, f32),
            pltpu.VMEM((GROUP, PACKS, 1, lines), f32),
            pltpu.VMEM((GROUP, PACKS, 1, lines), f32),
            pltpu.VMEM((PACKS, 1, lines), f32),
            pltpu.VMEM((GROUP, PACKS, 1, lines), f32),
            pltpu.VMEM((GROUP, 2, 1, lines), f32),
            pltpu.VMEM((GROUP, 2, 1, lines), f32),
            pltpu.SemaphoreType.REGULAR((3,)),
            pltpu.SemaphoreType.REGULAR((2,)),
            pltpu.SemaphoreType.DMA((5,)),
            pltpu.SemaphoreType.DMA((2, 2)),
            pltpu.SemaphoreType.DMA((2, 2)),
            pltpu.SemaphoreType.DMA((2, GROUP)),
            pltpu.SemaphoreType.DMA((2, GROUP)),
            pltpu.SemaphoreType.DMA((2, GROUP)),
        ],
        compiler_params=pltpu.CompilerParams(collective_id=0, has_side_effects=True),
        name="sweep",
    )(
        jacobian.reshape((nv, nv, points, lines)),
        state.reshape((nv, points, lines)),
        metric.reshape((points, lines)),
        dissipation.reshape((points, lines)),
        time_term.reshape((points, lines)),
    )
    return update.reshape(state.shape)


def solution(mesh):
    return jax.shard_map(
        per_device,
        mesh=mesh,
        in_specs=(
            P(None, None, "span", "line", None),
            P(None, "span", "line", None),
            P("span", "line", None),
            P("span", "line", None),
            P("span", "line", None),
        ),
        out_specs=P(None, "span", "line", None),
        check_vma=False,
    )
```

```python
import jax
import jax.numpy as jnp
from jax import lax
from jax.experimental import pallas as pl
from jax.experimental.pallas import tpu as pltpu
from jax.sharding import PartitionSpec as P

MESH = pl.DeviceIdType.MESH
f32 = jnp.float32
span_weight = 0.25
NV = 5
GROUP = 8
WIDE = 16
PACKS = 15
PAIRS = [(i, j) for i in range(NV) for j in range(i, NV)]
SYM = [[PAIRS.index((min(i, j), max(i, j))) for j in range(NV)] for i in range(NV)]
NSYM = len(PAIRS)


def roll(x, shift, axis):
    return pltpu.roll(x, shift, axis)


def mm(left, right):
    out = []
    for i in range(NV):
        acc = left[i][0][None] * right[0]
        for k in range(1, NV):
            acc = acc + left[i][k][None] * right[k]
        out.append(acc)
    return out


def inverse(m):
    m = [list(row) for row in m]
    for p in range(NV):
        r = 1.0 / m[p][p]
        for j in range(NV):
            if j != p:
                m[p][j] = m[p][j] * r
        for i in range(NV):
            if i != p:
                f = m[i][p]
                for j in range(NV):
                    if j != p:
                        m[i][j] = m[i][j] - f * m[p][j]
                m[i][p] = -(f * r)
        m[p][p] = r
    return m


def matvec(columns, v):
    acc = columns[0] * v[0][None]
    for k in range(1, NV):
        acc = acc + columns[k] * v[k][None]
    return acc


def tree_up_matrices(seg, la_ref, fb_ref, keep):
    def body(level, carry):
        back = GROUP - lax.shift_left(jnp.int32(1), level)
        fa = [seg[0, i] for i in range(NV)]
        la = [seg[1, i] for i in range(NV)]
        fb = [roll(x, back, 1) for x in fa]
        lb = [roll(x, back, 1) for x in la]
        t = mm([[la[i][NV + k] for k in range(NV)] for i in range(NV)], fb)
        eye = [[(1.0 if i == k else 0.0) - t[i][k] for k in range(NV)] for i in range(NV)]
        x = inverse(eye)
        q = [jnp.concatenate([la[i][0:NV], -t[i][NV:]], axis=0) for i in range(NV)]
        ela = mm(x, q)
        r = mm([[fb[i][k] for k in range(NV)] for i in range(NV)], ela)
        efb = [jnp.concatenate([-r[i][0:NV], fb[i][NV:] - r[i][NV:]], axis=0) for i in range(NV)]
        s = mm([[fa[i][NV + k] for k in range(NV)] for i in range(NV)], efb)
        y = mm([[lb[i][k] for k in range(NV)] for i in range(NV)], ela)
        for i in range(NV):
            for k in range(NV):
                keep[level, 0, k, i] = la[i][NV + k]
                keep[level, 1, k, i] = x[i][k]
                keep[level, 2, k, i] = fb[i][k]
                keep[level, 3, k, i] = fa[i][NV + k]
                keep[level, 4, k, i] = lb[i][k]
            la_ref[level, i, 0 : 2 * NV] = ela[i]
            fb_ref[level, i, 0 : 2 * NV] = efb[i]
            seg[0, i, 0:NV] = fa[i][0:NV] - s[i][0:NV]
            seg[0, i, NV:] = -s[i][NV:]
            seg[1, i, 0:NV] = -y[i][0:NV]
            seg[1, i, NV:] = lb[i][NV:] - y[i][NV:]
        return carry

    lax.fori_loop(0, 3, body, 0)


def tree_up_rhs(f, l, la_ref, fb_ref, keep):
    for level in range(3):
        back = GROUP - (1 << level)
        m = [[keep[level, w, k] for k in range(NV)] for w in range(5)]
        fb = roll(f, back, 1)
        lb = roll(l, back, 1)
        la_c = matvec(m[1], l - matvec(m[0], fb))
        fb_c = fb - matvec(m[2], la_c)
        f = f - matvec(m[3], fb_c)
        l = lb - matvec(m[4], la_c)
        for i in range(NV):
            la_ref[level, i, 2 * NV] = la_c[i]
            fb_ref[level, i, 2 * NV] = fb_c[i]
    return f, l


def spread(ref, index, column):
    return jnp.broadcast_to(
        ref[index + (column // 8, slice(column % 8, column % 8 + 1), slice(None))], (GROUP, 128)
    )


def tree_up_lanes(seg, near, temp, la_ref, fb_ref):
    tile = lax.broadcasted_iota(jnp.int32, (2, GROUP, 128), 0)
    column = tile * GROUP + lax.broadcasted_iota(jnp.int32, (2, GROUP, 128), 1)
    not_n = (column < NV) | (column == 2 * NV)
    not_p = column >= NV

    def body(level, carry):
        back = 128 - lax.shift_left(jnp.int32(WIDE), level)
        fa = [seg[0, i] for i in range(NV)]
        la = [seg[1, i] for i in range(NV)]
        fb = [roll(x, back, 2) for x in fa]
        lb = [roll(x, back, 2) for x in la]
        for i in range(NV):
            near[0, i] = fb[i]
            near[1, i] = lb[i]
        left = lambda ref, which, first: [
            [spread(ref, (which, i), first + k) for k in range(NV)] for i in range(NV)
        ]
        t = mm(left(seg, 1, NV), fb)
        for i in range(NV):
            temp[i] = t[i]
        eye = [
            [(1.0 if i == k else 0.0) - spread(temp, (i,), k) for k in range(NV)]
            for i in range(NV)
        ]
        x = inverse(eye)
        ela = mm(
            x, [jnp.where(not_n, la[i], 0.0) - jnp.where(not_p, t[i], 0.0) for i in range(NV)]
        )
        r = mm(left(near, 0, 0), ela)
        efb = [jnp.where(not_p, fb[i], 0.0) - r[i] for i in range(NV)]
        s = mm(left(seg, 0, NV), efb)
        y = mm(left(near, 1, 0), ela)
        for i in range(NV):
            la_ref[level, i] = ela[i]
            fb_ref[level, i] = efb[i]
            seg[0, i] = jnp.where(not_n, fa[i], 0.0) - s[i]
            seg[1, i] = jnp.where(not_p, lb[i], 0.0) - y[i]
        return carry

    lax.fori_loop(0, 3, body, 0)


def tree_down(p, n, la, fb, axis, base, pos):
    for level in (2, 1, 0):
        shift = base << level
        second = (pos & shift) != 0
        value = []
        for get in (la, fb):
            rows = []
            for i in range(NV):
                row = get(level, i, 2 * NV)
                if p is not None:
                    terms = [get(level, i, k) * p[k] for k in range(NV)]
                    terms += [get(level, i, NV + k) * n[k] for k in range(NV)]
                    while len(terms) > 1:
                        terms = [
                            terms[j] + terms[j + 1] if j + 1 < len(terms) else terms[j]
                            for j in range(0, len(terms), 2)
                        ]
                    row = row - terms[0]
                rows.append(row)
            value.append(rows)
        new_p = []
        new_n = []
        for i in range(NV):
            new_p.append(
                jnp.where(second, roll(value[0][i], shift, axis), 0.0 if p is None else p[i])
            )
            new_n.append(
                jnp.where(second, 0.0 if n is None else roll(n[i], shift, axis), value[1][i])
            )
        p, n = new_p, new_n
    return p, n


def swap_blocks(x):
    sub = lax.broadcasted_iota(jnp.int32, x.shape, 1)
    lane = lax.broadcasted_iota(jnp.int32, x.shape, 2)
    for bit in range(3):
        j = lax.shift_right_logical(sub, bit) & 1
        k = lax.shift_right_logical(lane, 4 + bit) & 1
        s = 1 << bit
        w = WIDE << bit
        up = roll(roll(x, GROUP - s, 1), w, 2)
        down = roll(roll(x, s, 1), 128 - w, 2)
        x = jnp.where(j == k, x, jnp.where(j == 0, up, down))
    return x


def kernel(
    jac_hbm, state_hbm, metric_hbm, diss_hbm, time_hbm, out_ref,
    jac_ref, state_ref, metric_ref, diss_ref, time_ref,
    sym_ref, flux_ref, fst, dst, xst, ls, us, fs,
    rim_out, rim_in, span_in,
    wc, pinv, hg, es,
    seg1, la1, fb1, keep, dev, part, ends, mean, small, seg2, la2, fb2, seg3, la3, fb3, near, temp,
    tmp, a_out, a_in, b_out, b_in, c_out, c_in,
    line_sem, plane_sem, load_sem, span_sem, rim_sem, a_sem, b_sem, c_sem,
):
    line = lax.axis_index("line")
    span = lax.axis_index("span")
    n_line = lax.axis_size("line")
    n_span = lax.axis_size("span")
    plane = line // GROUP
    member = line % GROUP
    line_next = lax.rem(line + 1, n_line)
    line_prev = lax.rem(line + n_line - 1, n_line)
    span_next = lax.rem(span + 1, n_span)
    span_prev = lax.rem(span + n_span - 1, n_span)
    far_first = sorted(range(1, GROUP), key=lambda o: abs(o - GROUP // 2))
    members = [plane * GROUP + lax.rem(member + o, GROUP) for o in range(1, GROUP)]
    planes = [lax.rem(plane + o, GROUP) * GROUP + member for o in range(1, GROUP)]

    loads = [
        pltpu.make_async_copy(source, target, load_sem.at[i])
        for i, (source, target) in enumerate(
            (
                (jac_hbm, jac_ref),
                (state_hbm, state_ref),
                (metric_hbm, metric_ref),
                (diss_hbm, diss_ref),
                (time_hbm, time_ref),
            )
        )
    ]
    for c in loads:
        c.start()

    peers = [(line, span_next), (line, span_prev), (line_next, span), (line_prev, span)]
    peers += [(planes[0], span), (planes[-1], span)]
    barrier = pltpu.get_barrier_semaphore()
    for peer in peers:
        pl.semaphore_signal(barrier, inc=1, device_id=peer, device_id_type=MESH)

    for c in loads:
        c.wait()
    metric = metric_ref[...]
    for q, (i, j) in enumerate(PAIRS):
        if i == j:
            value = jac_ref[i, i].astype(f32)
        else:
            value = 0.5 * (jac_ref[i, j].astype(f32) + jac_ref[j, i].astype(f32))
        sym_ref[q] = metric * value
    for i in range(NV):
        acc = sym_ref[SYM[i][0]] * state_ref[0]
        for k in range(1, NV):
            acc = acc + sym_ref[SYM[i][k]] * state_ref[k]
        flux_ref[i] = acc
    points = metric.shape[0]
    for side, row in ((0, points - 1), (1, 0)):
        for q in range(NSYM):
            rim_out[side, q : q + 1, :] = sym_ref[q, row : row + 1, :]
        for i in range(NV):
            rim_out[side, NSYM + i : NSYM + i + 1, :] = flux_ref[i, row : row + 1, :]
        rim_out[side, NSYM + NV : NSYM + NV + 1, :] = diss_ref[row : row + 1, :]
        rim_out[side, NSYM + NV + 1 :, :] = jnp.zeros((24 - NSYM - NV - 1, 128), f32)

    pl.semaphore_wait(barrier, len(peers))

    def greet(sem, size, step, position, spread_by, round_at):
        reach = (1 << round_at)
        for other in (lax.rem(position + reach, size), lax.rem(position + size - reach, size)):
            pl.semaphore_signal(
                sem.at[round_at], inc=1, device_id=(other * step + spread_by, span),
                device_id_type=MESH,
            )

    def greet_line(round_at):
        greet(line_sem, n_line, 1, line, 0, round_at)

    def greet_plane(round_at):
        greet(plane_sem, n_line // GROUP, GROUP, plane, member, round_at)

    greet_line(0)
    greet_plane(0)

    copies_rim = []
    for side, target in ((0, line_next), (1, line_prev)):
        copies_rim.append(
            pltpu.make_async_remote_copy(
                src_ref=rim_out.at[side], dst_ref=rim_in.at[side],
                send_sem=rim_sem.at[0, side], recv_sem=rim_sem.at[1, side],
                device_id=(target, span), device_id_type=MESH,
            )
        )
        copies_rim[-1].start()
    copies_span = []
    for side, target in ((0, span_next), (1, span_prev)):
        copies_span.append(
            pltpu.make_async_remote_copy(
                src_ref=state_hbm, dst_ref=span_in.at[side],
                send_sem=span_sem.at[0, side], recv_sem=span_sem.at[1, side],
                device_id=(line, target), device_id_type=MESH,
            )
        )
        copies_span[-1].start()

    for t in range(GROUP):
        fst[t + 1] = sym_ref[:, pl.ds(t, GROUP, stride=GROUP), :]
        xst[t + 1] = flux_ref[:, pl.ds(t, GROUP, stride=GROUP), :]
        dst[t + 1] = diss_ref[pl.ds(t, GROUP, stride=GROUP), :]
    sub2 = lax.broadcasted_iota(jnp.int32, (GROUP, 128), 0)
    sub3 = lax.broadcasted_iota(jnp.int32, (1, GROUP, 128), 1)
    fst[0] = roll(fst[GROUP], 1, 1)
    fst[GROUP + 1] = roll(fst[1], GROUP - 1, 1)
    dst[0] = roll(dst[GROUP], 1, 0)
    dst[GROUP + 1] = roll(dst[1], GROUP - 1, 0)

    def faces(t, carry):
        g = 0.25 * (fst[t] + fst[t + 1])
        f = 0.5 * (dst[t] + dst[t + 1])
        fs[t] = f
        for i in range(NV):
            for k in range(NV):
                e = g[SYM[i][k]]
                us[t, i, k] = e - f if i == k else e
                ls[t, i, k] = -e - f if i == k else -e
        return carry

    lax.fori_loop(0, GROUP + 1, faces, 0)

    for t in range(GROUP):
        dst[t] = fs[t] + time_ref[pl.ds(t, GROUP, stride=GROUP), :] + fs[t + 1]

    first_row = sub2 == 0
    last_row = sub2 == GROUP - 1
    scale = 1.0 / dst[0]
    for i in range(NV):
        for k in range(NV):
            same = 1.0 if i == k else 0.0
            wc[1, i, k] = jnp.where(first_row, -same, ls[0, i, k] * scale)
            wc[1, i, NV + k] = jnp.where(first_row, 0.0, us[1, i, k] * scale)
            pinv[0, k, i] = jnp.where(first_row, 0.0, same * scale)

    def forward(t, carry):
        diag = dst[t]
        low = [[ls[t, i, k] for k in range(NV)] for i in range(NV)]
        prod = mm(low, [wc[t, i] for i in range(NV)])
        m = [
            [(diag - prod[i][NV + k]) if i == k else -prod[i][NV + k] for k in range(NV)]
            for i in range(NV)
        ]
        inv = inverse(m)
        for i in range(NV):
            for k in range(NV):
                pinv[t, k, i] = inv[i][k]
        w = mm(inv, [-prod[i][0:NV] for i in range(NV)])
        c = mm(inv, [us[t + 1, i] for i in range(NV)])
        for i in range(NV):
            wc[t + 1, i, 0:NV] = w[i]
            wc[t + 1, i, NV:] = c[i]
        return carry

    lax.fori_loop(1, GROUP, forward, 0)
    for i in range(NV):
        for k in range(NV):
            same = 1.0 if i == k else 0.0
            wc[GROUP, i, k] = jnp.where(last_row, 0.0, wc[GROUP, i, k])
            wc[GROUP, i, NV + k] = jnp.where(last_row, -same, wc[GROUP, i, NV + k])
            pinv[GROUP - 1, k, i] = jnp.where(last_row, 0.0, pinv[GROUP - 1, k, i])
    pl.semaphore_wait(line_sem.at[0], 2)
    pl.semaphore_wait(plane_sem.at[0], 2)
    greet_line(1)
    greet_plane(1)

    for i in range(NV):
        hg[GROUP - 1, i] = wc[GROUP, i]

    def spikes(step, carry):
        t = GROUP - 2 - step
        c = [[wc[t + 1, i, NV + k] for k in range(NV)] for i in range(NV)]
        prod = mm(c, [hg[t + 1, i] for i in range(NV)])
        for i in range(NV):
            hg[t, i, 0:NV] = wc[t + 1, i, 0:NV] - prod[i][0:NV]
            hg[t, i, NV:] = -prod[i][NV:]
        return carry

    lax.fori_loop(0, GROUP - 1, spikes, 0)
    pl.semaphore_wait(line_sem.at[1], 2)
    greet_line(2)

    for i in range(NV):
        seg1[0, i] = jnp.where(sub3 == 0, hg[1, i], hg[0, i])
        seg1[1, i] = jnp.where(sub3 == GROUP - 1, hg[GROUP - 2, i], hg[GROUP - 1, i])
    tree_up_matrices(seg1, la1, fb1, keep)

    for which in range(2):
        for i in range(NV):
            dev[which, i] = jnp.zeros((2, GROUP, 128), f32)
            for c in range(2 * NV):
                dev[which, i, c // 8, c % 8 : c % 8 + 1, :] = seg1[which, i, c, 0:1, :]
    everywhere = lambda row: jnp.broadcast_to(row, (GROUP, 128))
    up_a = [[everywhere(us[1, i, k, 0:1, :]) for k in range(NV)] for i in range(NV)]
    low_z = [
        [everywhere(ls[GROUP - 1, i, k, GROUP - 1 :, :]) for k in range(NV)] for i in range(NV)
    ]
    prod_a = mm(up_a, [dev[0, i] for i in range(NV)])
    prod_z = mm(low_z, [dev[1, i] for i in range(NV)])
    for i in range(NV):
        part[0, i] = prod_a[i]
        part[1, i] = prod_z[i]
        ends[0, i] = jnp.zeros((2, GROUP, 128), f32)
        ends[1, i] = jnp.zeros((2, GROUP, 128), f32)

    for c in copies_rim:
        c.wait()
    rim_prev = jnp.where(line == 0, 0.0, rim_in[0])
    rim_next = jnp.where(line == n_line - 1, 0.0, rim_in[1])
    mean[0] = 0.25 * (rim_prev + rim_out[1])
    mean[1] = 0.25 * (rim_next + rim_out[0])
    for i in range(NV):
        for k in range(NV):
            for which in range(2):
                q = SYM[i][k]
                e = mean[which, q : q + 1, :]
                e = -e if which == 0 else e
                if i == k:
                    e = e - 2.0 * mean[which, NSYM + NV : NSYM + NV + 1, :]
                c = k + which * NV
                ends[which, i, c // 8, c % 8 : c % 8 + 1, :] = e
    for i in range(NV):
        xst[0, i] = jnp.where(
            first_row, rim_prev[NSYM + i : NSYM + i + 1, :], roll(xst[GROUP, i], 1, 0)
        )
        xst[GROUP + 1, i] = jnp.where(
            last_row, rim_next[NSYM + i : NSYM + i + 1, :], roll(xst[1, i], GROUP - 1, 0)
        )
    diag_a = everywhere(
        time_ref[0:1, :] + 2.0 * mean[0, NSYM + NV : NSYM + NV + 1, :] + fs[1, 0:1, :]
    )
    diag_z = everywhere(
        time_ref[points - 1 :, :]
        + fs[GROUP - 1, GROUP - 1 :, :]
        + 2.0 * mean[1, NSYM + NV : NSYM + NV + 1, :]
    )
    column = lax.broadcasted_iota(jnp.int32, (2, GROUP, 128), 0) * GROUP
    column = column + lax.broadcasted_iota(jnp.int32, (2, GROUP, 128), 1)
    is_p = column < NV
    inv_a = inverse(
        [
            [(diag_a if i == k else 0.0) - spread(part, (0, i), k) for k in range(NV)]
            for i in range(NV)
        ]
    )
    row_a = mm(inv_a, [jnp.where(is_p, ends[0, i], -prod_a[i]) for i in range(NV)])
    low_elem = [[spread(part, (1, i), k) for k in range(NV)] for i in range(NV)]
    cross = mm(low_elem, row_a)
    for i in range(NV):
        part[2, i] = row_a[i]
        part[3, i] = cross[i] - prod_z[i]
    inv_z = inverse(
        [
            [(diag_z if i == k else 0.0) + spread(part, (3, i), NV + k) for k in range(NV)]
            for i in range(NV)
        ]
    )
    end_z = mm(inv_z, [jnp.where(is_p, cross[i], ends[1, i]) for i in range(NV)])
    mix = [[spread(part, (2, i), NV + k) for k in range(NV)] for i in range(NV)]
    through = mm(mix, end_z)
    end_a = [jnp.where(is_p, row_a[i], 0.0) - through[i] for i in range(NV)]
    for i in range(NV):
        for k in range(NV):
            small[0, i, k] = inv_a[i][k]
            small[1, i, k] = inv_z[i][k]
        dev[0, i] = end_a[i]
        dev[1, i] = end_z[i]

    pl.semaphore_wait(line_sem.at[2], 2)
    pl.semaphore_wait(plane_sem.at[1], 2)
    for c in copies_span:
        c.wait()
    no_prev = span == 0
    no_next = span == n_span - 1
    d = jnp.zeros((NV, GROUP, 128), f32)
    for t in range(GROUP):
        rows = pl.ds(t, GROUP, stride=GROUP)
        before = jnp.where(no_prev, 0.0, span_in[0, :, rows, :])
        after = jnp.where(no_next, 0.0, span_in[1, :, rows, :])
        rhs = -0.5 * (xst[t + 2] - xst[t])
        rhs = rhs + span_weight * (after - 2.0 * state_ref[:, rows, :] + before)
        if t == 0:
            rhs_a = rhs
        if t == GROUP - 1:
            rhs_z = roll(rhs, 1, 1)
        for k in range(NV):
            rhs = rhs - ls[t, k] * d[k][None]
        d = pinv[t, 0] * rhs[0][None]
        for k in range(1, NV):
            d = d + pinv[t, k] * rhs[k][None]
        es[t] = d
    e = d
    for t in range(GROUP - 2, -1, -1):
        rows = [
            es[t, i] - jnp.sum(wc[t + 1, i, NV:] * e, axis=0) for i in range(NV)
        ]
        for i in range(NV):
            es[t, i] = rows[i]
        e = es[t]

    first, last = tree_up_rhs(
        jnp.where(sub3 == 0, es[1], es[0]),
        jnp.where(sub3 == GROUP - 1, es[GROUP - 2], es[GROUP - 1]),
        la1, fb1, keep,
    )

    def apply(matrix, vector):
        out = []
        for i in range(NV):
            acc = matrix(i, 0) * vector[0]
            for k in range(1, NV):
                acc = acc + matrix(i, k) * vector[k]
            out.append(acc)
        return out

    first = apply(lambda i, k: everywhere(us[1, i, k, 0:1, :]), first)
    last = apply(lambda i, k: everywhere(ls[GROUP - 1, i, k, GROUP - 1 :, :]), last)
    part_a = apply(lambda i, k: small[0, i, k], [rhs_a[i] - first[i] for i in range(NV)])
    carried = apply(lambda i, k: spread(part, (1, i), k), part_a)
    value_z = apply(
        lambda i, k: small[1, i, k], [rhs_z[i] - last[i] + carried[i] for i in range(NV)]
    )
    back = apply(lambda i, k: spread(part, (2, i), NV + k), value_z)
    value_a = [part_a[i] - back[i] for i in range(NV)]
    for which, value in ((0, value_a), (1, value_z)):
        for i in range(NV):
            dev[which, i, 1, 2:3, :] = value[i][0:1, :]

    def two_port_load(seg, landed):
        for s in range(GROUP):
            for r in range(PACKS):
                tmp[r, s : s + 1, :] = landed[s, r]
        packed = swap_blocks(tmp[...])
        for i in range(NV):
            seg[0, i, 0] = packed[i]
            seg[1, i, 0] = packed[NV + i]
            seg[0, i, 1] = packed[2 * NV + i]
            seg[1, i, 1] = roll(packed[2 * NV + i], GROUP - 3, 0)

    def pack(seg):
        return swap_blocks(
            jnp.concatenate(
                [seg[0, :, 0], seg[1, :, 0]]
                + [
                    jnp.where(sub2 < 3, seg[0, i, 1], roll(seg[1, i, 1], 3, 0))[None]
                    for i in range(NV)
                ],
                axis=0,
            )
        )

    packed = pack(dev)
    for s in range(GROUP):
        for r in range(PACKS):
            a_out[s, r] = packed[r, s : s + 1, :]
    copies = []
    for o in far_first:
        copies.append(
            pltpu.make_async_remote_copy(
                src_ref=a_out.at[lax.rem(member + o, GROUP)], dst_ref=a_in.at[member],
                send_sem=a_sem.at[0, o], recv_sem=a_sem.at[1, o],
                device_id=(members[o - 1], span), device_id_type=MESH,
            )
        )
        copies[-1].start()
    a_in[member] = a_out[member]
    for c in copies:
        c.wait()
    two_port_load(seg2, a_in)
    tree_up_lanes(seg2, near, temp, la2, fb2)

    packed = pack(seg2)
    for r in range(PACKS):
        b_out[r] = packed[r, 0:1, :]
    copies = []
    for o in far_first:
        copies.append(
            pltpu.make_async_remote_copy(
                src_ref=b_out, dst_ref=b_in.at[plane],
                send_sem=b_sem.at[0, o], recv_sem=b_sem.at[1, o],
                device_id=(planes[o - 1], span), device_id_type=MESH,
            )
        )
        copies[-1].start()
    b_in[plane] = b_out[...]
    for c in copies:
        c.wait()
    two_port_load(seg3, b_in)
    tree_up_lanes(seg3, near, temp, la3, fb3)

    lane = lax.broadcasted_iota(jnp.int32, (GROUP, 128), 1)
    get = lambda ref: lambda level, i, column: spread(ref, (level, i), column)
    p, n = tree_down(None, None, get(la3), get(fb3), 1, WIDE, lane)
    own = lax.rem(128 - plane * WIDE, 128)
    p = [roll(x, own, 1) for x in p]
    n = [roll(x, own, 1) for x in n]
    p, n = tree_down(p, n, get(la2), get(fb2), 1, WIDE, lane)

    for r, values in ((0, p), (1, n)):
        tile = values[0]
        for i in range(1, NV):
            tile = jnp.where(sub2 == i, values[i], tile)
        tmp[r] = tile
    packed = swap_blocks(tmp[0:2])
    for s in range(GROUP):
        for r in range(2):
            c_out[s, r] = packed[r, s : s + 1, :]
    copies = []
    for o in far_first:
        copies.append(
            pltpu.make_async_remote_copy(
                src_ref=c_out.at[lax.rem(member + o, GROUP)], dst_ref=c_in.at[member],
                send_sem=c_sem.at[0, o], recv_sem=c_sem.at[1, o],
                device_id=(members[o - 1], span), device_id_type=MESH,
            )
        )
        copies[-1].start()
    c_in[member] = c_out[member]
    for c in copies:
        c.wait()
    for s in range(GROUP):
        for r in range(2):
            tmp[r, s : s + 1, :] = c_in[s, r]
    packed = swap_blocks(tmp[0:2])
    p = [jnp.broadcast_to(packed[0, i : i + 1, :], (GROUP, 128)) for i in range(NV)]
    n = [jnp.broadcast_to(packed[1, i : i + 1, :], (GROUP, 128)) for i in range(NV)]
    ends_of = []
    for which in range(2):
        rows = []
        for i in range(NV):
            terms = [spread(dev, (which, i), k) * p[k] for k in range(NV)]
            terms += [spread(dev, (which, i), NV + k) * n[k] for k in range(NV)]
            while len(terms) > 1:
                terms = [
                    terms[j] + terms[j + 1] if j + 1 < len(terms) else terms[j]
                    for j in range(0, len(terms), 2)
                ]
            rows.append(spread(dev, (which, i), 2 * NV) - terms[0])
        ends_of.append(rows)
    p, n = ends_of
    get = lambda ref: lambda level, i, column: ref[level, i, column]
    p, n = tree_down(p, n, get(la1), get(fb1), 0, 1, sub2)
    pn = jnp.concatenate([x[None] for x in p + n], axis=0)
    for t in range(GROUP):
        for i in range(NV):
            out_ref[i, pl.ds(t, GROUP, stride=GROUP), :] = es[t, i] - jnp.sum(
                hg[t, i] * pn, axis=0
            )


def per_device(jacobian, state, metric, dissipation, time_term):
    nv = state.shape[0]
    points, lines = metric.shape[1:]
    vmem = pl.BlockSpec(memory_space=pltpu.VMEM)
    tile = (GROUP, lines)

    update = pl.pallas_call(
        kernel,
        out_shape=pltpu.VMEM((nv, points, lines), f32),
        in_specs=[pl.BlockSpec(memory_space=pl.ANY)] * 5,
        out_specs=vmem,
        scratch_shapes=[
            pltpu.VMEM((nv, nv, points, lines), jacobian.dtype),
            pltpu.VMEM((nv, points, lines), f32),
            pltpu.VMEM((points, lines), f32),
            pltpu.VMEM((points, lines), f32),
            pltpu.VMEM((points, lines), f32),
            pltpu.VMEM((NSYM, points, lines), f32),
            pltpu.VMEM((nv, points, lines), f32),
            pltpu.VMEM((GROUP + 2, NSYM) + tile, f32),
            pltpu.VMEM((GROUP + 2,) + tile, f32),
            pltpu.VMEM((GROUP + 2, nv) + tile, f32),
            pltpu.VMEM((GROUP + 1, nv, nv) + tile, f32),
            pltpu.VMEM((GROUP + 1, nv, nv) + tile, f32),
            pltpu.VMEM((GROUP + 1,) + tile, f32),
            pltpu.VMEM((2, 24, lines), f32),
            pltpu.VMEM((2, 24, lines), f32),
            pltpu.VMEM((2, nv, points, lines), f32),
            pltpu.VMEM((GROUP + 1, nv, 2 * nv) + tile, f32),
            pltpu.VMEM((GROUP, nv, nv) + tile, f32),
            pltpu.VMEM((GROUP, nv, 2 * nv) + tile, f32),
            pltpu.VMEM((GROUP, nv) + tile, f32),
            pltpu.VMEM((2, nv, 2 * nv) + tile, f32),
            pltpu.VMEM((3, nv, 2 * nv + 1) + tile, f32),
            pltpu.VMEM((3, nv, 2 * nv + 1) + tile, f32),
            pltpu.VMEM((3, 5, nv, nv) + tile, f32),
            pltpu.VMEM((2, nv, 2) + tile, f32),
            pltpu.VMEM((4, nv, 2) + tile, f32),
            pltpu.VMEM((2, nv, 2) + tile, f32),
            pltpu.VMEM((2, 24, lines), f32),
            pltpu.VMEM((2, nv, nv) + tile, f32),
            pltpu.VMEM((2, nv, 2) + tile, f32),
            pltpu.VMEM((3, nv, 2) + tile, f32),
            pltpu.VMEM((3, nv, 2) + tile, f32),
            pltpu.VMEM((2, nv, 2) + tile, f32),
            pltpu.VMEM((3, nv, 2) + tile, f32),
            pltpu.VMEM((3, nv, 2) + tile, f32),
            pltpu.VMEM((2, nv, 2) + tile, f32),
            pltpu.VMEM((nv, 2) + tile, f32),
            pltpu.VMEM((PACKS,) + tile, f32),
            pltpu.VMEM((GROUP, PACKS, 1, lines), f32),
            pltpu.VMEM((GROUP, PACKS, 1, lines), f32),
            pltpu.VMEM((PACKS, 1, lines), f32),
            pltpu.VMEM((GROUP, PACKS, 1, lines), f32),
            pltpu.VMEM((GROUP, 2, 1, lines), f32),
            pltpu.VMEM((GROUP, 2, 1, lines), f32),
            pltpu.SemaphoreType.REGULAR((3,)),
            pltpu.SemaphoreType.REGULAR((2,)),
            pltpu.SemaphoreType.DMA((5,)),
            pltpu.SemaphoreType.DMA((2, 2)),
            pltpu.SemaphoreType.DMA((2, 2)),
            pltpu.SemaphoreType.DMA((2, GROUP)),
            pltpu.SemaphoreType.DMA((2, GROUP)),
            pltpu.SemaphoreType.DMA((2, GROUP)),
        ],
        compiler_params=pltpu.CompilerParams(collective_id=0, has_side_effects=True),
        name="sweep",
    )(
        jacobian.reshape((nv, nv, points, lines)),
        state.reshape((nv, points, lines)),
        metric.reshape((points, lines)),
        dissipation.reshape((points, lines)),
        time_term.reshape((points, lines)),
    )
    return update.reshape(state.shape)


def solution(mesh):
    return jax.shard_map(
        per_device,
        mesh=mesh,
        in_specs=(
            P(None, None, "span", "line", None),
            P(None, "span", "line", None),
            P("span", "line", None),
            P("span", "line", None),
            P("span", "line", None),
        ),
        out_specs=P(None, "span", "line", None),
        check_vma=False,
    )
```

```python
import jax
import jax.numpy as jnp
from jax import lax
from jax.experimental import pallas as pl
from jax.experimental.pallas import tpu as pltpu
from jax.sharding import PartitionSpec as P

MESH = pl.DeviceIdType.MESH
f32 = jnp.float32
span_weight = 0.25
NV = 5
GROUP = 8
WIDE = 16
PACKS = 15
PAIRS = [(i, j) for i in range(NV) for j in range(i, NV)]
SYM = [[PAIRS.index((min(i, j), max(i, j))) for j in range(NV)] for i in range(NV)]
NSYM = len(PAIRS)


def roll(x, shift, axis):
    return pltpu.roll(x, shift, axis)


def mm(left, right):
    out = []
    for i in range(NV):
        acc = left[i][0][None] * right[0]
        for k in range(1, NV):
            acc = acc + left[i][k][None] * right[k]
        out.append(acc)
    return out


def inverse(m):
    m = [list(row) for row in m]
    for p in range(NV):
        r = 1.0 / m[p][p]
        for j in range(NV):
            if j != p:
                m[p][j] = m[p][j] * r
        for i in range(NV):
            if i != p:
                f = m[i][p]
                for j in range(NV):
                    if j != p:
                        m[i][j] = m[i][j] - f * m[p][j]
                m[i][p] = -(f * r)
        m[p][p] = r
    return m


def matvec(columns, v):
    acc = columns[0] * v[0][None]
    for k in range(1, NV):
        acc = acc + columns[k] * v[k][None]
    return acc


def tree_up_matrices(seg, la_ref, fb_ref, keep):
    def body(level, carry):
        back = GROUP - lax.shift_left(jnp.int32(1), level)
        fa = [seg[0, i] for i in range(NV)]
        la = [seg[1, i] for i in range(NV)]
        fb = [roll(x, back, 1) for x in fa]
        lb = [roll(x, back, 1) for x in la]
        t = mm([[la[i][NV + k] for k in range(NV)] for i in range(NV)], fb)
        eye = [[(1.0 if i == k else 0.0) - t[i][k] for k in range(NV)] for i in range(NV)]
        x = inverse(eye)
        q = [jnp.concatenate([la[i][0:NV], -t[i][NV:]], axis=0) for i in range(NV)]
        ela = mm(x, q)
        r = mm([[fb[i][k] for k in range(NV)] for i in range(NV)], ela)
        efb = [jnp.concatenate([-r[i][0:NV], fb[i][NV:] - r[i][NV:]], axis=0) for i in range(NV)]
        s = mm([[fa[i][NV + k] for k in range(NV)] for i in range(NV)], efb)
        y = mm([[lb[i][k] for k in range(NV)] for i in range(NV)], ela)
        for i in range(NV):
            for k in range(NV):
                keep[level, 0, k, i] = la[i][NV + k]
                keep[level, 1, k, i] = x[i][k]
                keep[level, 2, k, i] = fb[i][k]
                keep[level, 3, k, i] = fa[i][NV + k]
                keep[level, 4, k, i] = lb[i][k]
            la_ref[level, i, 0 : 2 * NV] = ela[i]
            fb_ref[level, i, 0 : 2 * NV] = efb[i]
            seg[0, i, 0:NV] = fa[i][0:NV] - s[i][0:NV]
            seg[0, i, NV:] = -s[i][NV:]
            seg[1, i, 0:NV] = -y[i][0:NV]
            seg[1, i, NV:] = lb[i][NV:] - y[i][NV:]
        return carry

    lax.fori_loop(0, 3, body, 0)


def tree_up_rhs(f, l, la_ref, fb_ref, keep):
    for level in range(3):
        back = GROUP - (1 << level)
        m = [[keep[level, w, k] for k in range(NV)] for w in range(5)]
        fb = roll(f, back, 1)
        lb = roll(l, back, 1)
        la_c = matvec(m[1], l - matvec(m[0], fb))
        fb_c = fb - matvec(m[2], la_c)
        f = f - matvec(m[3], fb_c)
        l = lb - matvec(m[4], la_c)
        for i in range(NV):
            la_ref[level, i, 2 * NV] = la_c[i]
            fb_ref[level, i, 2 * NV] = fb_c[i]
    return f, l


def spread(ref, index, column):
    return jnp.broadcast_to(
        ref[index + (column // 8, slice(column % 8, column % 8 + 1), slice(None))], (GROUP, 128)
    )


def tree_up_lanes(seg, near, temp, la_ref, fb_ref):
    tile = lax.broadcasted_iota(jnp.int32, (2, GROUP, 128), 0)
    column = tile * GROUP + lax.broadcasted_iota(jnp.int32, (2, GROUP, 128), 1)
    not_n = (column < NV) | (column == 2 * NV)
    not_p = column >= NV

    def body(level, carry):
        back = 128 - lax.shift_left(jnp.int32(WIDE), level)
        fa = [seg[0, i] for i in range(NV)]
        la = [seg[1, i] for i in range(NV)]
        fb = [roll(x, back, 2) for x in fa]
        lb = [roll(x, back, 2) for x in la]
        for i in range(NV):
            near[0, i] = fb[i]
            near[1, i] = lb[i]
        left = lambda ref, which, first: [
            [spread(ref, (which, i), first + k) for k in range(NV)] for i in range(NV)
        ]
        t = mm(left(seg, 1, NV), fb)
        for i in range(NV):
            temp[i] = t[i]
        eye = [
            [(1.0 if i == k else 0.0) - spread(temp, (i,), k) for k in range(NV)]
            for i in range(NV)
        ]
        x = inverse(eye)
        ela = mm(
            x, [jnp.where(not_n, la[i], 0.0) - jnp.where(not_p, t[i], 0.0) for i in range(NV)]
        )
        r = mm(left(near, 0, 0), ela)
        efb = [jnp.where(not_p, fb[i], 0.0) - r[i] for i in range(NV)]
        s = mm(left(seg, 0, NV), efb)
        y = mm(left(near, 1, 0), ela)
        for i in range(NV):
            la_ref[level, i] = ela[i]
            fb_ref[level, i] = efb[i]
            seg[0, i] = jnp.where(not_n, fa[i], 0.0) - s[i]
            seg[1, i] = jnp.where(not_p, lb[i], 0.0) - y[i]
        return carry

    lax.fori_loop(0, 3, body, 0)


def tree_down(p, n, la, fb, axis, base, pos):
    for level in (2, 1, 0):
        shift = base << level
        second = (pos & shift) != 0
        value = []
        for get in (la, fb):
            rows = []
            for i in range(NV):
                row = get(level, i, 2 * NV)
                if p is not None:
                    terms = [get(level, i, k) * p[k] for k in range(NV)]
                    terms += [get(level, i, NV + k) * n[k] for k in range(NV)]
                    while len(terms) > 1:
                        terms = [
                            terms[j] + terms[j + 1] if j + 1 < len(terms) else terms[j]
                            for j in range(0, len(terms), 2)
                        ]
                    row = row - terms[0]
                rows.append(row)
            value.append(rows)
        new_p = []
        new_n = []
        for i in range(NV):
            new_p.append(
                jnp.where(second, roll(value[0][i], shift, axis), 0.0 if p is None else p[i])
            )
            new_n.append(
                jnp.where(second, 0.0 if n is None else roll(n[i], shift, axis), value[1][i])
            )
        p, n = new_p, new_n
    return p, n


def swap_blocks(x):
    sub = lax.broadcasted_iota(jnp.int32, x.shape, 1)
    lane = lax.broadcasted_iota(jnp.int32, x.shape, 2)
    for bit in range(3):
        j = lax.shift_right_logical(sub, bit) & 1
        k = lax.shift_right_logical(lane, 4 + bit) & 1
        s = 1 << bit
        w = WIDE << bit
        up = roll(roll(x, GROUP - s, 1), w, 2)
        down = roll(roll(x, s, 1), 128 - w, 2)
        x = jnp.where(j == k, x, jnp.where(j == 0, up, down))
    return x


def kernel(
    jac_hbm, state_hbm, metric_hbm, diss_hbm, time_hbm, out_ref,
    jac_ref, state_ref, metric_ref, diss_ref, time_ref,
    sym_ref, flux_ref, fst, dst, xst, ls, us, fs,
    rim_out, rim_in, span_in,
    wc, pinv, hg, es,
    seg1, la1, fb1, keep, dev, part, ends, mean, small, seg2, la2, fb2, seg3, la3, fb3, near, temp,
    tmp, a_out, a_in, b_out, b_in, c_out, c_in,
    line_sem, plane_sem, load_sem, span_sem, rim_sem, a_sem, b_sem, c_sem,
):
    line = lax.axis_index("line")
    span = lax.axis_index("span")
    n_line = lax.axis_size("line")
    n_span = lax.axis_size("span")
    plane = line // GROUP
    member = line % GROUP
    line_next = lax.rem(line + 1, n_line)
    line_prev = lax.rem(line + n_line - 1, n_line)
    span_next = lax.rem(span + 1, n_span)
    span_prev = lax.rem(span + n_span - 1, n_span)
    far_first = sorted(range(1, GROUP), key=lambda o: abs(o - GROUP // 2))
    members = [plane * GROUP + lax.rem(member + o, GROUP) for o in range(1, GROUP)]
    planes = [lax.rem(plane + o, GROUP) * GROUP + member for o in range(1, GROUP)]

    pairs = [(metric_hbm, metric_ref), (diss_hbm, diss_ref), (time_hbm, time_ref)]
    pairs += [(jac_hbm.at[i], jac_ref.at[i]) for i in range(NV)]
    pairs += [(state_hbm.at[i], state_ref.at[i]) for i in range(NV)]
    loads = [
        pltpu.make_async_copy(source, target, load_sem.at[i])
        for i, (source, target) in enumerate(pairs)
    ]
    for c in loads:
        c.start()

    peers = [(line, span_next), (line, span_prev), (line_next, span), (line_prev, span)]
    peers += [(planes[0], span), (planes[-1], span)]
    barrier = pltpu.get_barrier_semaphore()
    for peer in peers:
        pl.semaphore_signal(barrier, inc=1, device_id=peer, device_id_type=MESH)

    for c in loads:
        c.wait()
    metric = metric_ref[...]
    for q, (i, j) in enumerate(PAIRS):
        if i == j:
            value = jac_ref[i, i].astype(f32)
        else:
            value = 0.5 * (jac_ref[i, j].astype(f32) + jac_ref[j, i].astype(f32))
        sym_ref[q] = metric * value
    for i in range(NV):
        acc = sym_ref[SYM[i][0]] * state_ref[0]
        for k in range(1, NV):
            acc = acc + sym_ref[SYM[i][k]] * state_ref[k]
        flux_ref[i] = acc
    points = metric.shape[0]
    for side, row in ((0, points - 1), (1, 0)):
        for q in range(NSYM):
            rim_out[side, q : q + 1, :] = sym_ref[q, row : row + 1, :]
        for i in range(NV):
            rim_out[side, NSYM + i : NSYM + i + 1, :] = flux_ref[i, row : row + 1, :]
        rim_out[side, NSYM + NV : NSYM + NV + 1, :] = diss_ref[row : row + 1, :]
        rim_out[side, NSYM + NV + 1 :, :] = jnp.zeros((24 - NSYM - NV - 1, 128), f32)

    for t in range(GROUP):
        fst[t + 1] = sym_ref[:, pl.ds(t, GROUP, stride=GROUP), :]
        xst[t + 1] = flux_ref[:, pl.ds(t, GROUP, stride=GROUP), :]
        dst[t + 1] = diss_ref[pl.ds(t, GROUP, stride=GROUP), :]
    sub2 = lax.broadcasted_iota(jnp.int32, (GROUP, 128), 0)
    sub3 = lax.broadcasted_iota(jnp.int32, (1, GROUP, 128), 1)
    fst[0] = roll(fst[GROUP], 1, 1)
    fst[GROUP + 1] = roll(fst[1], GROUP - 1, 1)
    dst[0] = roll(dst[GROUP], 1, 0)
    dst[GROUP + 1] = roll(dst[1], GROUP - 1, 0)

    def faces(t, carry):
        g = 0.25 * (fst[t] + fst[t + 1])
        f = 0.5 * (dst[t] + dst[t + 1])
        fs[t] = f
        for i in range(NV):
            for k in range(NV):
                e = g[SYM[i][k]]
                us[t, i, k] = e - f if i == k else e
                ls[t, i, k] = -e - f if i == k else -e
        return carry

    lax.fori_loop(0, GROUP + 1, faces, 0)

    pl.semaphore_wait(barrier, len(peers))

    def greet(sem, size, step, position, spread_by, round_at):
        reach = (1 << round_at)
        for other in (lax.rem(position + reach, size), lax.rem(position + size - reach, size)):
            pl.semaphore_signal(
                sem.at[round_at], inc=1, device_id=(other * step + spread_by, span),
                device_id_type=MESH,
            )

    def greet_line(round_at):
        greet(line_sem, n_line, 1, line, 0, round_at)

    def greet_plane(round_at):
        greet(plane_sem, n_line // GROUP, GROUP, plane, member, round_at)

    greet_line(0)
    greet_plane(0)

    copies_rim = []
    for side, target in ((0, line_next), (1, line_prev)):
        copies_rim.append(
            pltpu.make_async_remote_copy(
                src_ref=rim_out.at[side], dst_ref=rim_in.at[side],
                send_sem=rim_sem.at[0, side], recv_sem=rim_sem.at[1, side],
                device_id=(target, span), device_id_type=MESH,
            )
        )
        copies_rim[-1].start()
    copies_span = []
    for side, target in ((0, span_next), (1, span_prev)):
        copies_span.append(
            pltpu.make_async_remote_copy(
                src_ref=state_hbm, dst_ref=span_in.at[side],
                send_sem=span_sem.at[0, side], recv_sem=span_sem.at[1, side],
                device_id=(line, target), device_id_type=MESH,
            )
        )
        copies_span[-1].start()


    for t in range(GROUP):
        dst[t] = fs[t] + time_ref[pl.ds(t, GROUP, stride=GROUP), :] + fs[t + 1]

    first_row = sub2 == 0
    last_row = sub2 == GROUP - 1
    scale = 1.0 / dst[0]
    for i in range(NV):
        for k in range(NV):
            same = 1.0 if i == k else 0.0
            wc[1, i, k] = jnp.where(first_row, -same, ls[0, i, k] * scale)
            wc[1, i, NV + k] = jnp.where(first_row, 0.0, us[1, i, k] * scale)
            pinv[0, k, i] = jnp.where(first_row, 0.0, same * scale)

    def forward(t, carry):
        diag = dst[t]
        low = [[ls[t, i, k] for k in range(NV)] for i in range(NV)]
        prod = mm(low, [wc[t, i] for i in range(NV)])
        m = [
            [(diag - prod[i][NV + k]) if i == k else -prod[i][NV + k] for k in range(NV)]
            for i in range(NV)
        ]
        inv = inverse(m)
        for i in range(NV):
            for k in range(NV):
                pinv[t, k, i] = inv[i][k]
        w = mm(inv, [-prod[i][0:NV] for i in range(NV)])
        c = mm(inv, [us[t + 1, i] for i in range(NV)])
        for i in range(NV):
            wc[t + 1, i, 0:NV] = w[i]
            wc[t + 1, i, NV:] = c[i]
        return carry

    lax.fori_loop(1, GROUP, forward, 0)
    for i in range(NV):
        for k in range(NV):
            same = 1.0 if i == k else 0.0
            wc[GROUP, i, k] = jnp.where(last_row, 0.0, wc[GROUP, i, k])
            wc[GROUP, i, NV + k] = jnp.where(last_row, -same, wc[GROUP, i, NV + k])
            pinv[GROUP - 1, k, i] = jnp.where(last_row, 0.0, pinv[GROUP - 1, k, i])

    for i in range(NV):
        hg[GROUP - 1, i] = wc[GROUP, i]

    def spikes(step, carry):
        t = GROUP - 2 - step
        c = [[wc[t + 1, i, NV + k] for k in range(NV)] for i in range(NV)]
        prod = mm(c, [hg[t + 1, i] for i in range(NV)])
        for i in range(NV):
            hg[t, i, 0:NV] = wc[t + 1, i, 0:NV] - prod[i][0:NV]
            hg[t, i, NV:] = -prod[i][NV:]
        return carry

    lax.fori_loop(0, GROUP - 1, spikes, 0)
    pl.semaphore_wait(line_sem.at[0], 2)
    pl.semaphore_wait(plane_sem.at[0], 2)
    greet_line(1)
    greet_plane(1)

    for i in range(NV):
        seg1[0, i] = jnp.where(sub3 == 0, hg[1, i], hg[0, i])
        seg1[1, i] = jnp.where(sub3 == GROUP - 1, hg[GROUP - 2, i], hg[GROUP - 1, i])
    tree_up_matrices(seg1, la1, fb1, keep)

    for which in range(2):
        for i in range(NV):
            dev[which, i] = jnp.zeros((2, GROUP, 128), f32)
            for c in range(2 * NV):
                dev[which, i, c // 8, c % 8 : c % 8 + 1, :] = seg1[which, i, c, 0:1, :]
    everywhere = lambda row: jnp.broadcast_to(row, (GROUP, 128))
    up_a = [[everywhere(us[1, i, k, 0:1, :]) for k in range(NV)] for i in range(NV)]
    low_z = [
        [everywhere(ls[GROUP - 1, i, k, GROUP - 1 :, :]) for k in range(NV)] for i in range(NV)
    ]
    prod_a = mm(up_a, [dev[0, i] for i in range(NV)])
    prod_z = mm(low_z, [dev[1, i] for i in range(NV)])
    for i in range(NV):
        part[0, i] = prod_a[i]
        part[1, i] = prod_z[i]
        ends[0, i] = jnp.zeros((2, GROUP, 128), f32)
        ends[1, i] = jnp.zeros((2, GROUP, 128), f32)

    pl.semaphore_wait(line_sem.at[1], 2)
    greet_line(2)
    for c in copies_rim:
        c.wait()
    rim_prev = jnp.where(line == 0, 0.0, rim_in[0])
    rim_next = jnp.where(line == n_line - 1, 0.0, rim_in[1])
    mean[0] = 0.25 * (rim_prev + rim_out[1])
    mean[1] = 0.25 * (rim_next + rim_out[0])
    for i in range(NV):
        for k in range(NV):
            for which in range(2):
                q = SYM[i][k]
                e = mean[which, q : q + 1, :]
                e = -e if which == 0 else e
                if i == k:
                    e = e - 2.0 * mean[which, NSYM + NV : NSYM + NV + 1, :]
                c = k + which * NV
                ends[which, i, c // 8, c % 8 : c % 8 + 1, :] = e
    for i in range(NV):
        xst[0, i] = jnp.where(
            first_row, rim_prev[NSYM + i : NSYM + i + 1, :], roll(xst[GROUP, i], 1, 0)
        )
        xst[GROUP + 1, i] = jnp.where(
            last_row, rim_next[NSYM + i : NSYM + i + 1, :], roll(xst[1, i], GROUP - 1, 0)
        )
    diag_a = everywhere(
        time_ref[0:1, :] + 2.0 * mean[0, NSYM + NV : NSYM + NV + 1, :] + fs[1, 0:1, :]
    )
    diag_z = everywhere(
        time_ref[points - 1 :, :]
        + fs[GROUP - 1, GROUP - 1 :, :]
        + 2.0 * mean[1, NSYM + NV : NSYM + NV + 1, :]
    )
    column = lax.broadcasted_iota(jnp.int32, (2, GROUP, 128), 0) * GROUP
    column = column + lax.broadcasted_iota(jnp.int32, (2, GROUP, 128), 1)
    is_p = column < NV
    inv_a = inverse(
        [
            [(diag_a if i == k else 0.0) - spread(part, (0, i), k) for k in range(NV)]
            for i in range(NV)
        ]
    )
    row_a = mm(inv_a, [jnp.where(is_p, ends[0, i], -prod_a[i]) for i in range(NV)])
    low_elem = [[spread(part, (1, i), k) for k in range(NV)] for i in range(NV)]
    cross = mm(low_elem, row_a)
    for i in range(NV):
        part[2, i] = row_a[i]
        part[3, i] = cross[i] - prod_z[i]
    inv_z = inverse(
        [
            [(diag_z if i == k else 0.0) + spread(part, (3, i), NV + k) for k in range(NV)]
            for i in range(NV)
        ]
    )
    end_z = mm(inv_z, [jnp.where(is_p, cross[i], ends[1, i]) for i in range(NV)])
    mix = [[spread(part, (2, i), NV + k) for k in range(NV)] for i in range(NV)]
    through = mm(mix, end_z)
    end_a = [jnp.where(is_p, row_a[i], 0.0) - through[i] for i in range(NV)]
    for i in range(NV):
        for k in range(NV):
            small[0, i, k] = inv_a[i][k]
            small[1, i, k] = inv_z[i][k]
        dev[0, i] = end_a[i]
        dev[1, i] = end_z[i]

    pl.semaphore_wait(line_sem.at[2], 2)
    pl.semaphore_wait(plane_sem.at[1], 2)
    for c in copies_span:
        c.wait()
    no_prev = span == 0
    no_next = span == n_span - 1
    d = jnp.zeros((NV, GROUP, 128), f32)
    for t in range(GROUP):
        rows = pl.ds(t, GROUP, stride=GROUP)
        before = jnp.where(no_prev, 0.0, span_in[0, :, rows, :])
        after = jnp.where(no_next, 0.0, span_in[1, :, rows, :])
        rhs = -0.5 * (xst[t + 2] - xst[t])
        rhs = rhs + span_weight * (after - 2.0 * state_ref[:, rows, :] + before)
        if t == 0:
            rhs_a = rhs
        if t == GROUP - 1:
            rhs_z = roll(rhs, 1, 1)
        for k in range(NV):
            rhs = rhs - ls[t, k] * d[k][None]
        d = pinv[t, 0] * rhs[0][None]
        for k in range(1, NV):
            d = d + pinv[t, k] * rhs[k][None]
        es[t] = d
    e = d
    for t in range(GROUP - 2, -1, -1):
        rows = [
            es[t, i] - jnp.sum(wc[t + 1, i, NV:] * e, axis=0) for i in range(NV)
        ]
        for i in range(NV):
            es[t, i] = rows[i]
        e = es[t]

    first, last = tree_up_rhs(
        jnp.where(sub3 == 0, es[1], es[0]),
        jnp.where(sub3 == GROUP - 1, es[GROUP - 2], es[GROUP - 1]),
        la1, fb1, keep,
    )

    def apply(matrix, vector):
        out = []
        for i in range(NV):
            acc = matrix(i, 0) * vector[0]
            for k in range(1, NV):
                acc = acc + matrix(i, k) * vector[k]
            out.append(acc)
        return out

    first = apply(lambda i, k: everywhere(us[1, i, k, 0:1, :]), first)
    last = apply(lambda i, k: everywhere(ls[GROUP - 1, i, k, GROUP - 1 :, :]), last)
    part_a = apply(lambda i, k: small[0, i, k], [rhs_a[i] - first[i] for i in range(NV)])
    carried = apply(lambda i, k: spread(part, (1, i), k), part_a)
    value_z = apply(
        lambda i, k: small[1, i, k], [rhs_z[i] - last[i] + carried[i] for i in range(NV)]
    )
    back = apply(lambda i, k: spread(part, (2, i), NV + k), value_z)
    value_a = [part_a[i] - back[i] for i in range(NV)]
    for which, value in ((0, value_a), (1, value_z)):
        for i in range(NV):
            dev[which, i, 1, 2:3, :] = value[i][0:1, :]

    def two_port_load(seg, landed):
        for s in range(GROUP):
            for r in range(PACKS):
                tmp[r, s : s + 1, :] = landed[s, r]
        packed = swap_blocks(tmp[...])
        for i in range(NV):
            seg[0, i, 0] = packed[i]
            seg[1, i, 0] = packed[NV + i]
            seg[0, i, 1] = packed[2 * NV + i]
            seg[1, i, 1] = roll(packed[2 * NV + i], GROUP - 3, 0)

    def pack(seg):
        return swap_blocks(
            jnp.concatenate(
                [seg[0, :, 0], seg[1, :, 0]]
                + [
                    jnp.where(sub2 < 3, seg[0, i, 1], roll(seg[1, i, 1], 3, 0))[None]
                    for i in range(NV)
                ],
                axis=0,
            )
        )

    packed = pack(dev)
    for s in range(GROUP):
        for r in range(PACKS):
            a_out[s, r] = packed[r, s : s + 1, :]
    copies = []
    for o in far_first:
        copies.append(
            pltpu.make_async_remote_copy(
                src_ref=a_out.at[lax.rem(member + o, GROUP)], dst_ref=a_in.at[member],
                send_sem=a_sem.at[0, o], recv_sem=a_sem.at[1, o],
                device_id=(members[o - 1], span), device_id_type=MESH,
            )
        )
        copies[-1].start()
    a_in[member] = a_out[member]
    for c in copies:
        c.wait()
    two_port_load(seg2, a_in)
    tree_up_lanes(seg2, near, temp, la2, fb2)

    packed = pack(seg2)
    for r in range(PACKS):
        b_out[r] = packed[r, 0:1, :]
    copies = []
    for o in far_first:
        copies.append(
            pltpu.make_async_remote_copy(
                src_ref=b_out, dst_ref=b_in.at[plane],
                send_sem=b_sem.at[0, o], recv_sem=b_sem.at[1, o],
                device_id=(planes[o - 1], span), device_id_type=MESH,
            )
        )
        copies[-1].start()
    b_in[plane] = b_out[...]
    for c in copies:
        c.wait()
    two_port_load(seg3, b_in)
    tree_up_lanes(seg3, near, temp, la3, fb3)

    lane = lax.broadcasted_iota(jnp.int32, (GROUP, 128), 1)
    get = lambda ref: lambda level, i, column: spread(ref, (level, i), column)
    p, n = tree_down(None, None, get(la3), get(fb3), 1, WIDE, lane)
    own = lax.rem(128 - plane * WIDE, 128)
    p = [roll(x, own, 1) for x in p]
    n = [roll(x, own, 1) for x in n]
    p, n = tree_down(p, n, get(la2), get(fb2), 1, WIDE, lane)

    for r, values in ((0, p), (1, n)):
        tile = values[0]
        for i in range(1, NV):
            tile = jnp.where(sub2 == i, values[i], tile)
        tmp[r] = tile
    packed = swap_blocks(tmp[0:2])
    for s in range(GROUP):
        for r in range(2):
            c_out[s, r] = packed[r, s : s + 1, :]
    copies = []
    for o in far_first:
        copies.append(
            pltpu.make_async_remote_copy(
                src_ref=c_out.at[lax.rem(member + o, GROUP)], dst_ref=c_in.at[member],
                send_sem=c_sem.at[0, o], recv_sem=c_sem.at[1, o],
                device_id=(members[o - 1], span), device_id_type=MESH,
            )
        )
        copies[-1].start()
    c_in[member] = c_out[member]
    for c in copies:
        c.wait()
    for s in range(GROUP):
        for r in range(2):
            tmp[r, s : s + 1, :] = c_in[s, r]
    packed = swap_blocks(tmp[0:2])
    p = [jnp.broadcast_to(packed[0, i : i + 1, :], (GROUP, 128)) for i in range(NV)]
    n = [jnp.broadcast_to(packed[1, i : i + 1, :], (GROUP, 128)) for i in range(NV)]
    ends_of = []
    for which in range(2):
        rows = []
        for i in range(NV):
            terms = [spread(dev, (which, i), k) * p[k] for k in range(NV)]
            terms += [spread(dev, (which, i), NV + k) * n[k] for k in range(NV)]
            while len(terms) > 1:
                terms = [
                    terms[j] + terms[j + 1] if j + 1 < len(terms) else terms[j]
                    for j in range(0, len(terms), 2)
                ]
            rows.append(spread(dev, (which, i), 2 * NV) - terms[0])
        ends_of.append(rows)
    p, n = ends_of
    get = lambda ref: lambda level, i, column: ref[level, i, column]
    p, n = tree_down(p, n, get(la1), get(fb1), 0, 1, sub2)
    pn = jnp.concatenate([x[None] for x in p + n], axis=0)
    for t in range(GROUP):
        for i in range(NV):
            out_ref[i, pl.ds(t, GROUP, stride=GROUP), :] = es[t, i] - jnp.sum(
                hg[t, i] * pn, axis=0
            )


def per_device(jacobian, state, metric, dissipation, time_term):
    nv = state.shape[0]
    points, lines = metric.shape[1:]
    vmem = pl.BlockSpec(memory_space=pltpu.VMEM)
    tile = (GROUP, lines)

    update = pl.pallas_call(
        kernel,
        out_shape=pltpu.VMEM((nv, points, lines), f32),
        in_specs=[pl.BlockSpec(memory_space=pl.ANY)] * 5,
        out_specs=vmem,
        scratch_shapes=[
            pltpu.VMEM((nv, nv, points, lines), jacobian.dtype),
            pltpu.VMEM((nv, points, lines), f32),
            pltpu.VMEM((points, lines), f32),
            pltpu.VMEM((points, lines), f32),
            pltpu.VMEM((points, lines), f32),
            pltpu.VMEM((NSYM, points, lines), f32),
            pltpu.VMEM((nv, points, lines), f32),
            pltpu.VMEM((GROUP + 2, NSYM) + tile, f32),
            pltpu.VMEM((GROUP + 2,) + tile, f32),
            pltpu.VMEM((GROUP + 2, nv) + tile, f32),
            pltpu.VMEM((GROUP + 1, nv, nv) + tile, f32),
            pltpu.VMEM((GROUP + 1, nv, nv) + tile, f32),
            pltpu.VMEM((GROUP + 1,) + tile, f32),
            pltpu.VMEM((2, 24, lines), f32),
            pltpu.VMEM((2, 24, lines), f32),
            pltpu.VMEM((2, nv, points, lines), f32),
            pltpu.VMEM((GROUP + 1, nv, 2 * nv) + tile, f32),
            pltpu.VMEM((GROUP, nv, nv) + tile, f32),
            pltpu.VMEM((GROUP, nv, 2 * nv) + tile, f32),
            pltpu.VMEM((GROUP, nv) + tile, f32),
            pltpu.VMEM((2, nv, 2 * nv) + tile, f32),
            pltpu.VMEM((3, nv, 2 * nv + 1) + tile, f32),
            pltpu.VMEM((3, nv, 2 * nv + 1) + tile, f32),
            pltpu.VMEM((3, 5, nv, nv) + tile, f32),
            pltpu.VMEM((2, nv, 2) + tile, f32),
            pltpu.VMEM((4, nv, 2) + tile, f32),
            pltpu.VMEM((2, nv, 2) + tile, f32),
            pltpu.VMEM((2, 24, lines), f32),
            pltpu.VMEM((2, nv, nv) + tile, f32),
            pltpu.VMEM((2, nv, 2) + tile, f32),
            pltpu.VMEM((3, nv, 2) + tile, f32),
            pltpu.VMEM((3, nv, 2) + tile, f32),
            pltpu.VMEM((2, nv, 2) + tile, f32),
            pltpu.VMEM((3, nv, 2) + tile, f32),
            pltpu.VMEM((3, nv, 2) + tile, f32),
            pltpu.VMEM((2, nv, 2) + tile, f32),
            pltpu.VMEM((nv, 2) + tile, f32),
            pltpu.VMEM((PACKS,) + tile, f32),
            pltpu.VMEM((GROUP, PACKS, 1, lines), f32),
            pltpu.VMEM((GROUP, PACKS, 1, lines), f32),
            pltpu.VMEM((PACKS, 1, lines), f32),
            pltpu.VMEM((GROUP, PACKS, 1, lines), f32),
            pltpu.VMEM((GROUP, 2, 1, lines), f32),
            pltpu.VMEM((GROUP, 2, 1, lines), f32),
            pltpu.SemaphoreType.REGULAR((3,)),
            pltpu.SemaphoreType.REGULAR((2,)),
            pltpu.SemaphoreType.DMA((3 + 2 * NV,)),
            pltpu.SemaphoreType.DMA((2, 2)),
            pltpu.SemaphoreType.DMA((2, 2)),
            pltpu.SemaphoreType.DMA((2, GROUP)),
            pltpu.SemaphoreType.DMA((2, GROUP)),
            pltpu.SemaphoreType.DMA((2, GROUP)),
        ],
        compiler_params=pltpu.CompilerParams(collective_id=0, has_side_effects=True),
        name="sweep",
    )(
        jacobian.reshape((nv, nv, points, lines)),
        state.reshape((nv, points, lines)),
        metric.reshape((points, lines)),
        dissipation.reshape((points, lines)),
        time_term.reshape((points, lines)),
    )
    return update.reshape(state.shape)


def solution(mesh):
    return jax.shard_map(
        per_device,
        mesh=mesh,
        in_specs=(
            P(None, None, "span", "line", None),
            P(None, "span", "line", None),
            P("span", "line", None),
            P("span", "line", None),
            P("span", "line", None),
        ),
        out_specs=P(None, "span", "line", None),
        check_vma=False,
    )
```
